32 devices in a mesh: dp: 4 (over y, x), seq: 2 (over core), mp: 4 (over z).
Axes of the slice: x: 2, y: 2, z: 4, core: 2. Of those that a mesh axis runs over, the one named last changes fastest.
Arguments:
- node_feats: bfloat16 [8, 512, 1024], P(('dp', 'seq'), 'mp'), may hold values from -6 to 6
- coords: bfloat16 [8, 3, 512], P(('dp', 'seq'), None, 'mp'), may hold values from -36 to 36
- neighbours: int32 [8, 512, 48], P(('dp', 'seq'), 'mp'), may hold values from 0 to 511, as said below
- counts: int32 [8], P(('dp', 'seq')), may hold values from 256 to 512, as said below
- w_near: bfloat16 [1024, 1024], replicated, may hold values from -0.1875 to 0.1875
- w_rbf: bfloat16 [16, 1024], replicated, may hold values from -3.59375 to 3.59375
- gen_gain: float32 [1024], replicated, may hold values from 0.1 to 1.9
- w_logit: bfloat16 [1024, 33], replicated, may hold values from -0.59765625 to 0.59765625
- embed_table: bfloat16 [33, 2560], replicated, may hold values from -6 to 6
- trunk_gain: float32 [2560], replicated, may hold values from 0.1 to 1.9
- w_up: bfloat16 [2560, 5120], P('seq', 'mp'), may hold values from -0.125 to 0.125
- w_down: bfloat16 [5120, 2560], P('mp', 'seq'), may hold values from -0.078125 to 0.078125
Outputs:
- trunk_out: bfloat16 [8, 512, 2560], P(('dp', 'seq'), 'mp')
The draws below stay inside these ranges and needn't reach their ends.
Inputs may be any that keep to these rules, and one draw needn't show every extreme that they name: `neighbours`: each index lies in the residue's own block of 128 residues or in the block just before or after it; the 48 indices of a residue are distinct. Residues of a backbone at positions counts[b] and beyond are padding.
All inputs are finite; a program needn't handle non-finite values.
Results may differ from the reference program's by a relative error of at most 0.013.
Values may be sent and summed in bfloat16 or wider, within the bound.
No kernel may reach another device: no remote copies, remote signals or barrier semaphores. Data moves between devices by JAX's collectives and lax.ppermute only.
A program may use at most 128 MiB of HBM per device.

```python
import jax
import jax.numpy as jnp
from jax import lax

D = 1024
E = 2560
FFH = 5120
VOCAB = 33
RBF = 16
K = 48
RES = 128
FF_DEV = 1280
L = 512
NB = 8
N_MP = 4


def draw_counts(key, part):
    values = jax.random.randint(key, (NB,), L // 2, L + 1, dtype=jnp.int32)
    values = values.at[0].set(L)
    return values.at[1].set(L // 2)


def draw_neighbours(key, part):
    window_len = 3 * RES
    position = jnp.arange(L, dtype=jnp.int32)
    window_start = (position // RES - 1) * RES
    offsets_row = jnp.arange(window_len, dtype=jnp.int32)
    candidate = window_start[:, None] + offsets_row[None, :]
    inside = (candidate >= 0) & (candidate < L)
    scores = jax.random.randint(key, (NB, L, window_len), 0, 1 << 20, dtype=jnp.int32)
    scores = scores * window_len + offsets_row
    scores = jnp.where(inside[None], scores, -1 - offsets_row)
    top_scores, chosen = lax.top_k(scores, K)
    picked = jnp.take_along_axis(jnp.broadcast_to(candidate, (NB, L, window_len)), chosen, axis=2)
    valid_pick = jnp.take_along_axis(jnp.broadcast_to(inside, (NB, L, window_len)), chosen, axis=2)
    return jnp.where(valid_pick, picked, position[None, :, None]).astype(jnp.int32)


def shard_levels(rng, extent, cuts, least, top_value):
    def one(dim, parts):
        heights = jax.random.uniform(jax.random.fold_in(jax.random.fold_in(rng, 6), dim), (parts,), jnp.float32, least / len(cuts), top_value / len(cuts))
        return jnp.repeat(jnp.exp(heights), extent[dim] // parts).reshape((-1,) + (1,) * (len(extent) - dim - 1))

    factor_of = one(*cuts[0])
    for cut in cuts[1:]:
        factor_of = factor_of * one(*cut)
    return factor_of


def bell_draw(own_key, dims, scale, limit, shards=(), kind=jnp.bfloat16):
    level = shard_levels(own_key, dims, shards, -0.22, 0.18) if shards else 1.0
    values = jax.random.normal(own_key, dims, jnp.float32) * scale * level
    return jnp.minimum(jnp.maximum(values, -limit), limit).astype(kind)


def setup_inputs(seed: int = 0) -> dict:
    splits = jax.random.split(jax.random.key(seed), 13)
    return {
        "node_feats": bell_draw(splits[0], (NB, L, D), 1.0, 6.0, ((0, 8), (1, 4))),
        "coords": bell_draw(splits[1], (NB, 3, L), 6.0, 36.0, ((0, 8), (2, 4))),
        "neighbours": draw_neighbours(jax.random.fold_in(splits[12], 71), 0),
        "counts": draw_counts(jax.random.fold_in(splits[12], 71), 0),
        "w_near": bell_draw(splits[4], (D, D), D ** -0.5, 0.1875),
        "w_rbf": bell_draw(splits[5], (RBF, D), 0.6, 3.59375),
        "gen_gain": jnp.clip(1.0 + 0.18 * jax.random.normal(splits[6], (D,), jnp.float32), 0.1, 1.9),
        "w_logit": bell_draw(splits[7], (D, VOCAB), 0.1, 0.59765625),
        "embed_table": bell_draw(splits[8], (VOCAB, E), 1.0, 6.0),
        "trunk_gain": jnp.clip(1.0 + 0.18 * jax.random.normal(splits[9], (E,), jnp.float32), 0.1, 1.9),
        "w_up": bell_draw(splits[10], (E, FFH), E ** -0.5, 0.125, ((0, 2), (1, 4))),
        "w_down": bell_draw(splits[11], (FFH, E), FFH ** -0.5, 0.078125, ((0, 4), (1, 2))),
    }


def layer_norm(values, gain_vec):
    centred = values - lax.optimization_barrier(jnp.mean(values, axis=-1, keepdims=True))
    spread = lax.optimization_barrier(jnp.mean(centred * centred, axis=-1, keepdims=True))
    return centred * lax.rsqrt(spread + 1e-05) * gain_vec

def radial_basis(distance, bins):
    centres = 2.0 + 20.0 / (bins - 1) * jnp.arange(bins, dtype=jnp.float32)
    scaled = (distance[..., None] - centres) / 1.25
    return jnp.exp(-scaled * scaled).astype(jnp.bfloat16)

def reference(node_feats, coords, neighbours, counts, w_near, w_rbf, gen_gain, w_logit, embed_table, trunk_gain, w_up, w_down):

    def one_backbone(bundle):
        node_rows, position_xyz, link_rows, residue_count = bundle
        near = jnp.dot(node_rows, w_near, preferred_element_type=jnp.float32).astype(jnp.bfloat16)
        flat_links = link_rows.reshape(-1).astype(jnp.int32)
        picked = jnp.take(near, flat_links, axis=0, mode='clip')
        other_xyz = jnp.take(position_xyz, flat_links, axis=1, mode='clip').astype(jnp.float32).reshape(3, L, K)
        offsets_xyz = position_xyz.astype(jnp.float32)[:, :, None] - other_xyz
        distance = jnp.sqrt(lax.optimization_barrier(jnp.sum(offsets_xyz * offsets_xyz, axis=0)))
        radial = radial_basis(distance, RBF).reshape(L * K, RBF)
        preact = jnp.dot(radial, w_rbf, preferred_element_type=jnp.float32) + picked.astype(jnp.float32)
        edge_act = jax.nn.gelu(preact, approximate=False)
        keep_mask = (flat_links < residue_count).astype(jnp.float32)
        message = lax.optimization_barrier(jnp.sum((edge_act * keep_mask[:, None]).reshape(L, K, D), axis=1)) / 30.0
        mixed_rows = layer_norm(node_rows.astype(jnp.float32) + message, gen_gain).astype(jnp.bfloat16)
        logits = jnp.dot(mixed_rows, w_logit, preferred_element_type=jnp.float32)
        bounded = 8.0 * jnp.tanh(logits / 8.0)
        exponent = jnp.exp(bounded)
        probability = (exponent / lax.optimization_barrier(jnp.sum(exponent, axis=-1, keepdims=True))).astype(jnp.bfloat16)
        valid_rows = (jnp.arange(L).astype(jnp.int32) < residue_count).astype(jnp.float32)
        soft_embed = (jnp.dot(probability, embed_table, preferred_element_type=jnp.float32) * valid_rows[:, None]).astype(jnp.bfloat16)
        normed = layer_norm(soft_embed.astype(jnp.float32), trunk_gain).astype(jnp.bfloat16)
        inner_act = jax.nn.gelu(jnp.dot(normed, w_up, preferred_element_type=jnp.float32), approximate=False).astype(jnp.bfloat16)
        total_sum = jnp.zeros((L, E), jnp.float32)
        for block_idx in range(N_MP):
            block_part = jnp.dot(inner_act[:, block_idx * FF_DEV:(block_idx + 1) * FF_DEV], w_down[block_idx * FF_DEV:(block_idx + 1) * FF_DEV], preferred_element_type=jnp.float32)
            total_sum = total_sum + lax.optimization_barrier(block_part.astype(jnp.bfloat16)).astype(jnp.float32)
        return (soft_embed.astype(jnp.float32) + total_sum).astype(jnp.bfloat16)
    return lax.map(one_backbone, (node_feats, coords, neighbours, counts))
```

```python
import functools

import jax
import jax.numpy as jnp
from jax import lax
from jax.experimental import pallas as pl
from jax.experimental.pallas import tpu as pltpu
from jax.sharding import PartitionSpec as P

F32 = jnp.float32
BF16 = jnp.bfloat16
LANES = 128
COORD_ROWS = 16


def swap(value, axis, step):
    count = lax.axis_size(axis)
    return lax.ppermute(value, axis, [(i, i ^ step) for i in range(count)])


def high_low(value):
    high = value.astype(BF16)
    low = (value - high.astype(F32)).astype(BF16)
    return high, low


def message_kernel(
    rows_at_once,
    vocab_size,
    own_ref,
    side_ref,
    other_ref,
    link_ref,
    scalar_ref,
    w_near_ref,
    w_rbf_ref,
    gain_ref,
    w_logit_ref,
    table_ref,
    soft_ref,
    coded_ref,
    window_ref,
    xyz_ref,
    message_ref,
):
    residues, neighbour_count = link_ref.shape
    feature_dim = w_near_ref.shape[0]
    bins = w_rbf_ref.shape[0]
    window = 3 * residues
    blocks = (own_ref, side_ref, other_ref)
    for slot, ref in enumerate(blocks):
        near = jnp.dot(ref[0:residues, :], w_near_ref[...], preferred_element_type=F32)
        window_ref[slot * residues : (slot + 1) * residues, :] = near.astype(BF16)
    window_ref[window : window + bins, :] = w_rbf_ref[...]
    window_ref[window + bins :, :] = jnp.zeros(
        (window_ref.shape[0] - window - bins, feature_dim), BF16
    )
    positions = [
        ref[residues : residues + COORD_ROWS, 0:residues].astype(F32) for ref in blocks
    ]
    xyz_ref[...] = jnp.transpose(
        jnp.concatenate([positions[0], jnp.zeros((LANES - COORD_ROWS, residues), F32)], axis=0)
    )
    block_index = scalar_ref[0]
    residue_count = scalar_ref[1]
    lane = lax.broadcasted_iota(jnp.int32, (rows_at_once, LANES), 1)
    centres = 2.0 + (20.0 / (bins - 1)) * lane.astype(F32)
    padding = jnp.zeros((rows_at_once, LANES - neighbour_count), jnp.int32)

    def one_chunk(step, carry):
        first = pl.multiple_of(step * rows_at_once, rows_at_once)
        links = jnp.concatenate([link_ref[pl.ds(first, rows_at_once), :], padding], axis=1)
        keep = (links < residue_count) & (lane < neighbour_count)
        within = jnp.bitwise_and(links, residues - 1)
        block_of = lax.shift_right_logical(links, residues.bit_length() - 1)
        side_block = jnp.bitwise_xor(block_index, 1)
        slot_of = jnp.where(
            block_of == block_index, 0, jnp.where(block_of == side_block, 1, 2)
        )
        own_xyz = xyz_ref[pl.ds(first, rows_at_once), :]
        squared = None
        for slot in range(3):
            total = None
            for axis in range(3):
                offset = own_xyz[:, axis : axis + 1] - positions[slot][axis : axis + 1, :]
                total = offset * offset if total is None else total + offset * offset
            picked = jnp.take_along_axis(total, within, axis=1)
            squared = picked if squared is None else jnp.where(slot_of == slot, picked, squared)
        distance = jnp.where(keep, jnp.sqrt(squared), 1e6)
        place = jnp.where(keep, within + slot_of * residues, -1)
        rows = []
        for k in range(neighbour_count):
            place_k = jnp.broadcast_to(place[:, k : k + 1], (rows_at_once, LANES))
            parts = [
                jnp.where(place_k == lane + slot * residues, 1.0, 0.0).astype(BF16)
                for slot in range(3)
            ]
            distance_k = jnp.broadcast_to(distance[:, k : k + 1], (rows_at_once, LANES))
            scaled = (distance_k - centres) * (1.0 / 1.25)
            radial = jnp.where(lane < bins, jnp.exp(-scaled * scaled), 0.0)
            parts.append(radial.astype(BF16))
            rows.append(jnp.concatenate(parts, axis=1))
        selector = jnp.concatenate(rows, axis=0)
        width = 256
        for column in range(feature_dim // width):
            cols = slice(column * width, (column + 1) * width)
            preact = jnp.dot(selector, window_ref[:, cols], preferred_element_type=F32)
            doubled = preact * (1.0 + lax.erf(preact * (0.5**0.5)))
            message_ref[pl.ds(first, rows_at_once), cols] = jnp.sum(
                doubled.reshape(neighbour_count, rows_at_once, width), axis=0
            ) * (0.5 / 30.0)
        return carry

    lax.fori_loop(0, residues // rows_at_once, one_chunk, 0)

    values = own_ref[0:residues, :].astype(F32) + message_ref[...]
    centred = values - jnp.mean(values, axis=1, keepdims=True)
    spread = jnp.mean(centred * centred, axis=1, keepdims=True)
    mixed = (centred * lax.rsqrt(spread + 1e-5) * gain_ref[...]).astype(BF16)
    logits = jnp.dot(mixed, w_logit_ref[...], preferred_element_type=F32)
    bounded = 8.0 * jnp.tanh(logits * 0.125)
    token = lax.broadcasted_iota(jnp.int32, logits.shape, 1)
    exponent = jnp.where(token < vocab_size, jnp.exp(bounded), 0.0)
    probability = (exponent / jnp.sum(exponent, axis=1, keepdims=True)).astype(BF16)
    residue = block_index * residues + lax.broadcasted_iota(jnp.int32, (residues, 1), 0)
    valid = (residue < residue_count).astype(F32)
    soft = (
        jnp.dot(probability, table_ref[...], preferred_element_type=F32) * valid
    ).astype(BF16)
    soft_ref[...] = soft
    soft_wide = soft.astype(F32)
    soft_centred = soft_wide - jnp.mean(soft_wide, axis=1, keepdims=True)
    soft_spread = jnp.mean(soft_centred * soft_centred, axis=1, keepdims=True)
    coded = probability.astype(F32) * (lax.rsqrt(soft_spread + 1e-5) * valid)
    high, low = high_low(coded)
    half = LANES // 2
    coded_ref[...] = jnp.concatenate([high[:, :half], low[:, :half]], axis=1)


def messages(own, side, other, links, scalars, w_near, w_rbf, gen_gain, w_logit, table, vocab):
    residues = links.shape[0]
    feature_dim = w_near.shape[0]
    embed_dim = table.shape[1]
    bins = w_rbf.shape[0]
    depth = -(-(3 * residues + bins) // 256) * 256
    in_vmem = pl.BlockSpec(memory_space=pltpu.VMEM)
    return pl.pallas_call(
        functools.partial(message_kernel, min(32, residues), vocab),
        out_shape=(
            jax.ShapeDtypeStruct((residues, embed_dim), BF16),
            jax.ShapeDtypeStruct((residues, LANES), BF16),
        ),
        in_specs=[in_vmem] * 4 + [pl.BlockSpec(memory_space=pltpu.SMEM)] + [in_vmem] * 5,
        out_specs=(in_vmem, in_vmem),
        scratch_shapes=[
            pltpu.VMEM((depth, feature_dim), BF16),
            pltpu.VMEM((residues, LANES), F32),
            pltpu.VMEM((residues, feature_dim), F32),
        ],
        compiler_params=pltpu.CompilerParams(vmem_limit_bytes=40 << 20),
        cost_estimate=pl.CostEstimate(
            flops=12_000_000_000, bytes_accessed=6_000_000, transcendentals=7_000_000
        ),
        name="messages",
    )(own, side, other, links, scalars, w_near, w_rbf, gen_gain, w_logit, table)


def on_device(
    node_feats,
    coords,
    neighbours,
    counts,
    w_near,
    w_rbf,
    gen_gain,
    w_logit,
    embed_table,
    trunk_gain,
    w_up,
    w_down,
):
    backbones, residues, feature_dim = node_feats.shape
    assert backbones == 1 and lax.axis_size("mp") == 4
    vocab_size, embed_dim = embed_table.shape
    half = LANES // 2
    seq_count = lax.axis_size("seq")
    seq_index = lax.axis_index("seq")
    block_index = lax.axis_index("mp")

    xyz = jnp.pad(coords[0], ((0, COORD_ROWS - 3), (0, feature_dim - residues)))
    own = jnp.concatenate([node_feats[0], xyz], axis=0)
    side = swap(own, "mp", 1)
    other = lax.ppermute(own, "mp", [(1, 2), (2, 1)])

    table_wide = embed_table.astype(F32)
    table_centred = table_wide - jnp.mean(table_wide, axis=1, keepdims=True)
    table_scaled = jnp.pad(
        (table_centred * trunk_gain).astype(BF16), ((0, half - vocab_size), (0, 0))
    )
    table_part = lax.dynamic_slice_in_dim(
        table_scaled, seq_index * w_up.shape[0], w_up.shape[0], 1
    )
    token_up = jnp.dot(table_part, w_up, preferred_element_type=F32)
    if seq_count == 2:
        token_up = token_up + swap(token_up, "seq", 1)
        down_parts = [w_down, swap(w_down, "seq", 1)]
    else:
        token_up = lax.psum(token_up, "seq")
        down_parts = [lax.all_gather(w_down, "seq", axis=1, tiled=True)]
    up_high, up_low = high_low(token_up)
    up_stack = jnp.concatenate([up_high, up_high, up_low, up_low], axis=0)

    scalars = jnp.stack([block_index.astype(jnp.int32), counts[0]])
    soft, coded = messages(
        own,
        side,
        other,
        neighbours[0],
        scalars,
        w_near,
        w_rbf,
        gen_gain[None, :],
        jnp.pad(w_logit, ((0, 0), (0, LANES - vocab_size))),
        jnp.pad(embed_table, ((0, LANES - vocab_size), (0, 0))),
        vocab_size,
    )

    coded_rows = [coded] + [swap(coded, "mp", step) for step in (1, 2, 3)]

    def inner_of(rows):
        wide = jnp.concatenate([rows, rows], axis=1)
        total = jnp.dot(wide, up_stack, preferred_element_type=F32)
        return jax.nn.gelu(total, approximate=False).astype(BF16)

    inner = [inner_of(rows) for rows in coded_rows]

    def product(step, part):
        return jnp.dot(inner[step], part, preferred_element_type=F32)

    inward = [(0, 1), (3, 2)]
    middle = [(1, 2), (2, 1)]
    outward = [(1, 0), (2, 3)]
    sums = []
    for part in down_parts:
        far_edge = lax.ppermute(product(3, part).astype(BF16), "mp", inward)
        far_near = lax.ppermute(product(2, part).astype(BF16), "mp", inward)
        to_inner = lax.ppermute(product(1, part).astype(BF16), "mp", inward)
        crossing_edge = lax.ppermute(
            (product(2, part) + far_edge.astype(F32)).astype(BF16), "mp", middle
        )
        crossing_near = lax.ppermute(
            (product(3, part) + far_near.astype(F32)).astype(BF16), "mp", middle
        )
        to_edge = lax.ppermute(
            (product(1, part) + crossing_edge.astype(F32)).astype(BF16), "mp", outward
        )
        sums.append(
            product(0, part)
            + to_inner.astype(F32)
            + crossing_near.astype(F32)
            + to_edge.astype(F32)
        )
    if seq_count == 2:
        first = seq_index == 0
        total = jnp.concatenate(
            [jnp.where(first, sums[0], sums[1]), jnp.where(first, sums[1], sums[0])], axis=1
        )
    else:
        total = sums[0]
    return (soft.astype(F32) + total).astype(BF16)[None]


def solution(mesh):
    placed = (
        P(("dp", "seq"), "mp", None),
        P(("dp", "seq"), None, "mp"),
        P(("dp", "seq"), "mp", None),
        P(("dp", "seq")),
        P(),
        P(),
        P(),
        P(),
        P(),
        P(),
        P("seq", "mp"),
        P("mp", "seq"),
    )
    return jax.shard_map(
        on_device,
        mesh=mesh,
        in_specs=placed,
        out_specs=P(("dp", "seq"), "mp", None),
        check_vma=False,
    )
```

```python
import functools

import jax
import jax.numpy as jnp
from jax import lax
from jax.experimental import pallas as pl
from jax.experimental.pallas import tpu as pltpu
from jax.sharding import PartitionSpec as P

F32 = jnp.float32
BF16 = jnp.bfloat16
LANES = 128
COORD_ROWS = 16


def swap(value, axis, step):
    count = lax.axis_size(axis)
    return lax.ppermute(value, axis, [(i, i ^ step) for i in range(count)])


def high_low(value):
    high = value.astype(BF16)
    low = (value - high.astype(F32)).astype(BF16)
    return high, low


def in_hbm(*arrays):
    return [pltpu.with_memory_space_constraint(array, pltpu.HBM) for array in arrays]


def near_kernel(feats_ref, xyz_ref, w_near_ref, out_ref, feats, xyz, weights, arrived):
    residues = feats.shape[0]
    parts, height, depth = weights.shape
    copies = [
        pltpu.make_async_copy(feats_ref, feats, arrived.at[parts]),
        pltpu.make_async_copy(xyz_ref, xyz, arrived.at[parts + 1]),
    ] + [
        pltpu.make_async_copy(
            w_near_ref.at[part * height : (part + 1) * height, :],
            weights.at[part],
            arrived.at[part],
        )
        for part in range(parts)
    ]
    for copy in copies:
        copy.start()
    out_ref[residues:, :] = jnp.zeros((COORD_ROWS, depth), BF16)
    copies[0].wait()
    copies[1].wait()
    out_ref[residues : residues + 3, 0:residues] = xyz[...]
    near = None
    for part in range(parts):
        copies[2 + part].wait()
        term = jnp.dot(
            feats[:, part * height : (part + 1) * height],
            weights[part],
            preferred_element_type=F32,
        )
        near = term if near is None else near + term
    out_ref[0:residues, :] = near.astype(BF16)


def near_rows(feats, xyz, w_near):
    residues, depth = feats.shape
    parts = 4
    return pl.pallas_call(
        near_kernel,
        out_shape=jax.ShapeDtypeStruct((residues + COORD_ROWS, depth), BF16),
        in_specs=[pl.BlockSpec(memory_space=pltpu.HBM)] * 3,
        out_specs=pl.BlockSpec(memory_space=pltpu.VMEM),
        scratch_shapes=[
            pltpu.VMEM(feats.shape, BF16),
            pltpu.VMEM(xyz.shape, BF16),
            pltpu.VMEM((parts, depth // parts, depth), BF16),
            pltpu.SemaphoreType.DMA((parts + 2,)),
        ],
        name="near_rows",
    )(*in_hbm(feats, xyz, w_near))


def message_kernel(
    rows_at_once,
    first_row,
    with_tokens,
    *refs,
):
    if with_tokens:
        (token_gain_ref, w_up_ref), refs = refs[9:11], refs[:9] + refs[11:]
        (token_ref,), refs = refs[12:13], refs[:12] + refs[13:]
        (token_gain_buf, w_up_buf, scaled_ref), refs = refs[-3:], refs[:-3]
    message_body(
        rows_at_once,
        first_row,
        (token_gain_ref, w_up_ref, token_ref, token_gain_buf, w_up_buf, scaled_ref)
        if with_tokens
        else None,
        *refs,
    )


def message_body(
    rows_at_once,
    first_row,
    tokens,
    own_ref,
    side_ref,
    other_ref,
    feats_ref,
    link_ref,
    w_rbf_ref,
    gain_ref,
    w_logit_ref,
    table_ref,
    scalar_ref,
    soft_ref,
    coded_ref,
    window_ref,
    position_ref,
    feats_buf,
    link_buf,
    gain_buf,
    w_logit_buf,
    table_buf,
    place_ref,
    xyz_ref,
    message_ref,
    soft_buf,
    arrived,
):
    neighbour_count, residues = link_ref.shape
    bins, feature_dim = w_rbf_ref.shape
    vocab_size = table_ref.shape[0]
    window = 3 * residues
    early = []
    for slot, ref in enumerate((own_ref, side_ref, other_ref)):
        early.append(
            (ref.at[0:residues, :], window_ref.at[slot * residues : (slot + 1) * residues, :])
        )
        early.append(
            (ref.at[residues : residues + COORD_ROWS, 0:residues], position_ref.at[slot])
        )
    early.append((w_rbf_ref, window_ref.at[window : window + bins, :]))
    early.append((link_ref, link_buf))
    late = [
        (feats_ref, feats_buf),
        (gain_ref, gain_buf),
        (w_logit_ref, w_logit_buf),
        (table_ref, table_buf),
    ]
    if tokens:
        token_gain_ref, w_up_ref, token_ref, token_gain_buf, w_up_buf, scaled_ref = tokens
        late += [(token_gain_ref, token_gain_buf), (w_up_ref, w_up_buf)]
    copies = [
        pltpu.make_async_copy(source, target, arrived.at[place])
        for place, (source, target) in enumerate(early + late)
    ]
    for copy in copies:
        copy.start()
    window_ref[window + bins :, :] = jnp.zeros(
        (window_ref.shape[0] - window - bins, feature_dim), BF16
    )
    for copy in copies[: len(early)]:
        copy.wait()

    block_index = scalar_ref[0]
    residue_count = scalar_ref[1]
    positions = [position_ref[slot].astype(F32) for slot in range(3)]
    xyz_ref[...] = jnp.transpose(
        jnp.concatenate([positions[0], jnp.zeros((LANES - COORD_ROWS, residues), F32)], axis=0)
    )
    place_ref[...] = jnp.transpose(
        jnp.concatenate(
            [link_buf[...], jnp.zeros((LANES - neighbour_count, residues), jnp.int32)], axis=0
        )
    )
    lane = lax.broadcasted_iota(jnp.int32, (rows_at_once, LANES), 1)
    centres = 2.0 + (20.0 / (bins - 1)) * lane.astype(F32)

    def one_chunk(step, carry):
        begin = pl.multiple_of(step * rows_at_once, rows_at_once)
        first = first_row + begin
        links = place_ref[pl.ds(first, rows_at_once), :]
        keep = (links < residue_count) & (lane < neighbour_count)
        within = jnp.bitwise_and(links, residues - 1)
        block_of = lax.shift_right_logical(links, residues.bit_length() - 1)
        side_block = jnp.bitwise_xor(block_index, 1)
        slot_of = jnp.where(
            block_of == block_index, 0, jnp.where(block_of == side_block, 1, 2)
        )
        own_xyz = xyz_ref[pl.ds(first, rows_at_once), :]
        squared = None
        for slot in range(3):
            total = None
            for axis in range(3):
                offset = own_xyz[:, axis : axis + 1] - positions[slot][axis : axis + 1, :]
                total = offset * offset if total is None else total + offset * offset
            picked = jnp.take_along_axis(total, within, axis=1)
            squared = picked if squared is None else jnp.where(slot_of == slot, picked, squared)
        distance = jnp.where(keep, jnp.sqrt(squared), 1e6)
        place = jnp.where(keep, within + slot_of * residues, -1)
        rows = []
        for k in range(neighbour_count):
            place_k = jnp.broadcast_to(place[:, k : k + 1], (rows_at_once, LANES))
            parts = [
                jnp.where(place_k == lane + slot * residues, 1.0, 0.0).astype(BF16)
                for slot in range(3)
            ]
            distance_k = jnp.broadcast_to(distance[:, k : k + 1], (rows_at_once, LANES))
            scaled = (distance_k - centres) * (1.0 / 1.25)
            radial = jnp.where(lane < bins, jnp.exp(-scaled * scaled), 0.0)
            parts.append(radial.astype(BF16))
            rows.append(jnp.concatenate(parts, axis=1))
        selector = jnp.concatenate(rows, axis=0)
        width = 256
        for column in range(feature_dim // width):
            cols = slice(column * width, (column + 1) * width)
            preact = jnp.dot(selector, window_ref[:, cols], preferred_element_type=F32)
            doubled = preact * (1.0 + lax.erf(preact * (0.5**0.5)))
            message_ref[pl.ds(begin, rows_at_once), cols] = jnp.sum(
                doubled.reshape(neighbour_count, rows_at_once, width), axis=0
            ) * (0.5 / 30.0)
        return carry

    count = message_ref.shape[0]
    lax.fori_loop(0, count // rows_at_once, one_chunk, 0)

    for copy in copies[len(early) :]:
        copy.wait()
    values = feats_buf[first_row : first_row + count, :].astype(F32) + message_ref[...]
    centred = values - jnp.mean(values, axis=1, keepdims=True)
    spread = jnp.mean(centred * centred, axis=1, keepdims=True)
    mixed = (centred * lax.rsqrt(spread + 1e-5) * gain_buf[...]).astype(BF16)
    half = LANES // 2
    w_logit = jnp.concatenate(
        [w_logit_buf[...].astype(F32), jnp.zeros((LANES - vocab_size, feature_dim), F32)], axis=0
    ).astype(BF16)
    logits = lax.dot_general(
        mixed, w_logit, (((1,), (1,)), ((), ())), preferred_element_type=F32
    )
    bounded = 8.0 * jnp.tanh(logits * 0.125)
    token = lax.broadcasted_iota(jnp.int32, logits.shape, 1)
    exponent = jnp.where(token < vocab_size, jnp.exp(bounded), 0.0)
    probability = (exponent / jnp.sum(exponent, axis=1, keepdims=True)).astype(BF16)
    residue = (
        block_index * residues + first_row + lax.broadcasted_iota(jnp.int32, (count, 1), 0)
    )
    valid = (residue < residue_count).astype(F32)
    table = jnp.concatenate(
        [
            table_buf[...].astype(F32),
            jnp.zeros((LANES - vocab_size, table_buf.shape[1]), F32),
        ],
        axis=0,
    ).astype(BF16)
    soft = (jnp.dot(probability, table, preferred_element_type=F32) * valid).astype(BF16)
    soft_buf[...] = soft
    leaving = pltpu.make_async_copy(soft_buf, soft_ref, arrived.at[len(copies)])
    leaving.start()
    soft_wide = soft.astype(F32)
    soft_centred = soft_wide - jnp.mean(soft_wide, axis=1, keepdims=True)
    soft_spread = jnp.mean(soft_centred * soft_centred, axis=1, keepdims=True)
    coded = probability.astype(F32) * (lax.rsqrt(soft_spread + 1e-5) * valid)
    high, low = high_low(coded)
    coded_ref[...] = jnp.concatenate([high[:, :half], low[:, :half]], axis=1)
    if tokens:
        wide = table.astype(F32)[:half]
        wide = wide - jnp.mean(wide, axis=1, keepdims=True)
        scaled_ref[...] = (wide * token_gain_buf[...]).astype(BF16)
        depth = w_up_buf.shape[0]
        part = scaled_ref[:, pl.ds(pl.multiple_of(scalar_ref[2] * depth, LANES), depth)]
        token_ref[...] = jnp.dot(part, w_up_buf[...], preferred_element_type=F32)
    leaving.wait()


def messages(own, side, other, feats, links, w_rbf, gain, w_logit, table, scalars, rows, tokens):
    residues, feature_dim = feats.shape
    embed_dim = table.shape[1]
    bins = w_rbf.shape[0]
    depth = -(-(3 * residues + bins) // 256) * 256
    count = rows[1] - rows[0]
    in_vmem = pl.BlockSpec(memory_space=pltpu.VMEM)
    in_hbm_spec = pl.BlockSpec(memory_space=pltpu.HBM)
    arrays = [own, side, other, feats, links, w_rbf, gain, w_logit, table, *tokens]
    out_shape = [pltpu.HBM((count, embed_dim), BF16), jax.ShapeDtypeStruct((count, LANES), BF16)]
    scratch = [
        pltpu.VMEM((depth, feature_dim), BF16),
        pltpu.VMEM((3, COORD_ROWS, residues), BF16),
        pltpu.VMEM(feats.shape, BF16),
        pltpu.VMEM(links.shape, jnp.int32),
        pltpu.VMEM(gain.shape, F32),
        pltpu.VMEM(w_logit.shape, BF16),
        pltpu.VMEM(table.shape, BF16),
        pltpu.VMEM((residues, LANES), jnp.int32),
        pltpu.VMEM((residues, LANES), F32),
        pltpu.VMEM((count, feature_dim), F32),
        pltpu.VMEM((count, embed_dim), BF16),
        pltpu.SemaphoreType.DMA((16,)),
    ]
    if tokens:
        token_gain, w_up = tokens
        out_shape.append(jax.ShapeDtypeStruct((LANES // 2, w_up.shape[1]), F32))
        scratch += [
            pltpu.VMEM(token_gain.shape, F32),
            pltpu.VMEM(w_up.shape, BF16),
            pltpu.VMEM((LANES // 2, embed_dim), BF16),
        ]
    return pl.pallas_call(
        functools.partial(message_kernel, min(32, count), rows[0], bool(tokens)),
        out_shape=out_shape,
        in_specs=[in_hbm_spec] * len(arrays) + [pl.BlockSpec(memory_space=pltpu.SMEM)],
        out_specs=[in_hbm_spec] + [in_vmem] * (len(out_shape) - 1),
        scratch_shapes=scratch,
        compiler_params=pltpu.CompilerParams(vmem_limit_bytes=20 << 20),
        cost_estimate=pl.CostEstimate(
            flops=100_000_000 * count, bytes_accessed=5_000_000, transcendentals=50_000 * count
        ),
        name="messages",
    )(*in_hbm(*arrays), scalars)


def gelu_rows(rows, up):
    total = jnp.dot(rows, jnp.concatenate([up, up], axis=0), preferred_element_type=F32)
    return (0.5 * total * (1.0 + lax.erf(total * (0.5**0.5)))).astype(BF16)


def trunk_kernel(columns, targets, *refs):
    coded, up_ref = refs[:4], refs[4]
    weights = refs[5 : 5 + len(columns)]
    outs = refs[5 + len(columns) : -5]
    buffer, inner, results, arrived, left = refs[-5:]
    chunk = buffer.shape[2]
    copies = [
        pltpu.make_async_copy(
            ref.at[:, first : first + chunk], buffer.at[place], arrived.at[place]
        )
        for place, (ref, first) in enumerate(zip(weights, columns))
    ]
    for copy in copies:
        copy.start()
    rows = coded[0].shape[0]
    for place, ref in enumerate(coded):
        inner[place * rows : (place + 1) * rows, :] = gelu_rows(ref[...], up_ref[...])
    leaving = []
    for place, copy in enumerate(copies):
        copy.wait()
        value = jnp.dot(inner[...], buffer[place], preferred_element_type=F32)
        results[place] = value.astype(BF16)
        for number, (start, stop) in enumerate(targets):
            leaving.append(
                pltpu.make_async_copy(
                    results.at[place, start:stop, :],
                    outs[number].at[:, place * chunk : (place + 1) * chunk],
                    left.at[len(leaving)],
                )
            )
            leaving[-1].start()
    for copy in leaving:
        copy.wait()


def trunk(coded, up, pieces, targets, chunk):
    rows, hidden = coded[0].shape[0], up.shape[1]
    in_vmem = pl.BlockSpec(memory_space=pltpu.VMEM)
    hbm_spec = pl.BlockSpec(memory_space=pltpu.HBM)
    return pl.pallas_call(
        functools.partial(trunk_kernel, [column for _, column in pieces], targets),
        out_shape=[
            pltpu.HBM((stop - start, len(pieces) * chunk), BF16) for start, stop in targets
        ],
        in_specs=[in_vmem] * 5 + [hbm_spec] * len(pieces),
        out_specs=[hbm_spec] * len(targets),
        scratch_shapes=[
            pltpu.VMEM((len(pieces), hidden, chunk), BF16),
            pltpu.VMEM((4 * rows, hidden), BF16),
            pltpu.VMEM((len(pieces), 4 * rows, chunk), BF16),
            pltpu.SemaphoreType.DMA((len(pieces),)),
            pltpu.SemaphoreType.DMA((len(pieces) * len(targets),)),
        ],
        compiler_params=pltpu.CompilerParams(vmem_limit_bytes=16 << 20),
        cost_estimate=pl.CostEstimate(
            flops=8 * rows * len(pieces) * hidden * chunk,
            bytes_accessed=2 * hidden * chunk * len(pieces),
            transcendentals=4 * rows * hidden,
        ),
        name="trunk",
    )(*coded, up, *in_hbm(*[array for array, _ in pieces]))


def rounded_sum(left, right):
    return (left.astype(F32) + right.astype(F32)).astype(BF16)


def on_device(
    node_feats,
    coords,
    neighbours,
    counts,
    w_near,
    w_rbf,
    gen_gain,
    w_logit,
    embed_table,
    trunk_gain,
    w_up,
    w_down,
):
    backbones, residues, feature_dim = node_feats.shape
    assert backbones == 1 and lax.axis_size("mp") == 4
    vocab_size, embed_dim = embed_table.shape
    half = LANES // 2
    seq_count = lax.axis_size("seq")
    seq_index = lax.axis_index("seq")
    block_index = lax.axis_index("mp")

    own = near_rows(node_feats[0], coords[0], w_near)
    side = swap(own, "mp", 1)
    other = lax.ppermute(own, "mp", [(1, 2), (2, 1)])

    scalars = jnp.stack([block_index.astype(jnp.int32), counts[0], seq_index.astype(jnp.int32)])

    def some_messages(first, last, tokens):
        return messages(
            own,
            side,
            other,
            node_feats[0],
            neighbours[0].T,
            w_rbf,
            gen_gain[None, :],
            w_logit.T,
            embed_table,
            scalars,
            (first, last),
            tokens,
        )

    if seq_count == 2 and w_up.shape[0] % LANES == 0:
        soft_a, coded_a, token_up = some_messages(
            0, residues // 2, (trunk_gain[None, :], w_up)
        )
        token_up = (token_up + swap(token_up, "seq", 1)).astype(BF16)
        whole = [w_down, swap(w_down, "seq", 1)]
    else:
        soft_a, coded_a = some_messages(0, residues // 2, ())
        table_wide = embed_table.astype(F32)
        table_centred = table_wide - jnp.mean(table_wide, axis=1, keepdims=True)
        table_scaled = jnp.pad(
            (table_centred * trunk_gain).astype(BF16), ((0, half - vocab_size), (0, 0))
        )
        table_part = lax.dynamic_slice_in_dim(
            table_scaled, seq_index * w_up.shape[0], w_up.shape[0], 1
        )
        token_up = lax.psum(
            jnp.dot(table_part, w_up, preferred_element_type=F32), "seq"
        ).astype(BF16)
        whole = [lax.all_gather(w_down, "seq", axis=1, tiled=True)]
    soft_b, coded_b = some_messages(residues // 2, residues, ())
    soft = jnp.concatenate([soft_a, soft_b], axis=0)
    chunk = embed_dim // 4
    pieces = [(part, first) for part in whole for first in range(0, part.shape[1], chunk)]

    part_rows = residues // 2
    inward = [(0, 1), (3, 2)]
    crossing = [(1, 2), (2, 1)]
    skipping = [(1, 3), (2, 0)]
    sums = []
    order = ()
    for coded in (coded_a, coded_b):
        coded_rows = [swap(coded, "mp", step) for step in (3, 2, 1)] + [coded]
        coded_rows, order = lax.optimization_barrier((coded_rows, order))
        far, near, held = trunk(
            coded_rows,
            token_up,
            pieces,
            [
                (0, 2 * part_rows),
                (2 * part_rows, 3 * part_rows),
                (3 * part_rows, 4 * part_rows),
            ],
            chunk,
        )
        arrived = lax.ppermute(far, "mp", inward)
        arrived, near = lax.optimization_barrier((arrived, near))
        swapped = swap(near, "mp", 1)
        across = rounded_sum(far[:part_rows], arrived[part_rows:])
        beyond = rounded_sum(far[part_rows:], arrived[:part_rows])
        order = (across, beyond)
        across = lax.ppermute(across, "mp", crossing)
        beyond = lax.ppermute(beyond, "mp", skipping)
        sums.append(
            held.astype(F32)
            + swapped.astype(F32)
            + across.astype(F32)
            + beyond.astype(F32)
        )
    total = jnp.concatenate(sums, axis=0)
    if len(whole) == 2:
        middle = embed_dim // 2
        turned = jnp.concatenate([total[:, middle:], total[:, :middle]], axis=1)
        total = jnp.where(seq_index == 0, total, turned)
    return (soft.astype(F32) + total).astype(BF16)[None]


def solution(mesh):
    placed = (
        P(("dp", "seq"), "mp", None),
        P(("dp", "seq"), None, "mp"),
        P(("dp", "seq"), "mp", None),
        P(("dp", "seq")),
        P(),
        P(),
        P(),
        P(),
        P(),
        P(),
        P("seq", "mp"),
        P("mp", "seq"),
    )
    return jax.shard_map(
        on_device,
        mesh=mesh,
        in_specs=placed,
        out_specs=P(("dp", "seq"), "mp", None),
        check_vma=False,
    )
```

```python
import functools

import jax
import jax.numpy as jnp
from jax import lax
from jax.experimental import pallas as pl
from jax.experimental.pallas import tpu as pltpu
from jax.sharding import PartitionSpec as P

F32 = jnp.float32
BF16 = jnp.bfloat16
LANES = 128
COORD_ROWS = 16


def swap(value, axis, step):
    count = lax.axis_size(axis)
    return lax.ppermute(value, axis, [(i, i ^ step) for i in range(count)])


def high_low(value):
    high = value.astype(BF16)
    low = (value - high.astype(F32)).astype(BF16)
    return high, low


def in_hbm(*arrays):
    return [pltpu.with_memory_space_constraint(array, pltpu.HBM) for array in arrays]


def near_kernel(feats_ref, xyz_ref, w_near_ref, out_ref, feats, xyz, weights, arrived):
    residues = feats.shape[0]
    parts, height, depth = weights.shape
    copies = [
        pltpu.make_async_copy(feats_ref, feats, arrived.at[parts]),
        pltpu.make_async_copy(xyz_ref, xyz, arrived.at[parts + 1]),
    ] + [
        pltpu.make_async_copy(
            w_near_ref.at[part * height : (part + 1) * height, :],
            weights.at[part],
            arrived.at[part],
        )
        for part in range(parts)
    ]
    for copy in copies:
        copy.start()
    out_ref[residues:, :] = jnp.zeros((COORD_ROWS, depth), BF16)
    copies[0].wait()
    copies[1].wait()
    out_ref[residues : residues + 3, 0:residues] = xyz[...]
    near = None
    for part in range(parts):
        copies[2 + part].wait()
        term = jnp.dot(
            feats[:, part * height : (part + 1) * height],
            weights[part],
            preferred_element_type=F32,
        )
        near = term if near is None else near + term
    out_ref[0:residues, :] = near.astype(BF16)


def near_rows(feats, xyz, w_near):
    residues, depth = feats.shape
    parts = 4
    return pl.pallas_call(
        near_kernel,
        out_shape=jax.ShapeDtypeStruct((residues + COORD_ROWS, depth), BF16),
        in_specs=[pl.BlockSpec(memory_space=pltpu.HBM)] * 3,
        out_specs=pl.BlockSpec(memory_space=pltpu.VMEM),
        scratch_shapes=[
            pltpu.VMEM(feats.shape, BF16),
            pltpu.VMEM(xyz.shape, BF16),
            pltpu.VMEM((parts, depth // parts, depth), BF16),
            pltpu.SemaphoreType.DMA((parts + 2,)),
        ],
        name="near_rows",
    )(*in_hbm(feats, xyz, w_near))


def message_kernel(
    rows_at_once,
    first_row,
    with_tokens,
    *refs,
):
    if with_tokens:
        (token_gain_ref, w_up_ref), refs = refs[9:11], refs[:9] + refs[11:]
        (token_ref,), refs = refs[12:13], refs[:12] + refs[13:]
        (token_gain_buf, w_up_buf, scaled_ref), refs = refs[-3:], refs[:-3]
    message_body(
        rows_at_once,
        first_row,
        (token_gain_ref, w_up_ref, token_ref, token_gain_buf, w_up_buf, scaled_ref)
        if with_tokens
        else None,
        *refs,
    )


def message_body(
    rows_at_once,
    first_row,
    tokens,
    own_ref,
    side_ref,
    other_ref,
    feats_ref,
    link_ref,
    w_rbf_ref,
    gain_ref,
    w_logit_ref,
    table_ref,
    scalar_ref,
    shown_ref,
    coded_ref,
    window_ref,
    position_ref,
    feats_buf,
    link_buf,
    gain_buf,
    w_logit_buf,
    table_buf,
    place_ref,
    xyz_ref,
    message_ref,
    arrived,
):
    neighbour_count, residues = link_ref.shape
    bins, feature_dim = w_rbf_ref.shape
    vocab_size = table_ref.shape[0]
    window = 3 * residues
    early = []
    for slot, ref in enumerate((own_ref, side_ref, other_ref)):
        early.append(
            (ref.at[0:residues, :], window_ref.at[slot * residues : (slot + 1) * residues, :])
        )
        early.append(
            (ref.at[residues : residues + COORD_ROWS, 0:residues], position_ref.at[slot])
        )
    early.append((w_rbf_ref, window_ref.at[window : window + bins, :]))
    early.append((link_ref, link_buf))
    late = [
        (feats_ref, feats_buf),
        (gain_ref, gain_buf),
        (w_logit_ref, w_logit_buf),
        (table_ref, table_buf),
    ]
    if tokens:
        token_gain_ref, w_up_ref, token_ref, token_gain_buf, w_up_buf, scaled_ref = tokens
        late += [(token_gain_ref, token_gain_buf), (w_up_ref, w_up_buf)]
    copies = [
        pltpu.make_async_copy(source, target, arrived.at[place])
        for place, (source, target) in enumerate(early + late)
    ]
    for copy in copies:
        copy.start()
    window_ref[window + bins :, :] = jnp.zeros(
        (window_ref.shape[0] - window - bins, feature_dim), BF16
    )
    for copy in copies[: len(early)]:
        copy.wait()

    block_index = scalar_ref[0]
    residue_count = scalar_ref[1]
    positions = [position_ref[slot].astype(F32) for slot in range(3)]
    xyz_ref[...] = jnp.transpose(
        jnp.concatenate([positions[0], jnp.zeros((LANES - COORD_ROWS, residues), F32)], axis=0)
    )
    place_ref[...] = jnp.transpose(
        jnp.concatenate(
            [link_buf[...], jnp.zeros((LANES - neighbour_count, residues), jnp.int32)], axis=0
        )
    )
    lane = lax.broadcasted_iota(jnp.int32, (rows_at_once, LANES), 1)
    centres = 2.0 + (20.0 / (bins - 1)) * lane.astype(F32)

    lane_short = lane.astype(jnp.int16)
    one, zero = jnp.ones((), BF16), jnp.zeros((), BF16)
    count = message_ref.shape[0]
    for begin in range(0, count, rows_at_once):
        first = first_row + begin
        links = place_ref[pl.ds(first, rows_at_once), :]
        keep = (links < residue_count) & (lane < neighbour_count)
        within = jnp.bitwise_and(links, residues - 1)
        block_of = lax.shift_right_logical(links, residues.bit_length() - 1)
        side_block = jnp.bitwise_xor(block_index, 1)
        slot_of = jnp.where(
            block_of == block_index, 0, jnp.where(block_of == side_block, 1, 2)
        )
        own_xyz = xyz_ref[pl.ds(first, rows_at_once), :]
        squared = None
        for slot in range(3):
            total = None
            for axis in range(3):
                offset = own_xyz[:, axis : axis + 1] - positions[slot][axis : axis + 1, :]
                total = offset * offset if total is None else total + offset * offset
            picked = jnp.take_along_axis(total, within, axis=1)
            squared = picked if squared is None else jnp.where(slot_of == slot, picked, squared)
        distance = jnp.where(keep, jnp.sqrt(squared), 1e6)
        place = jnp.where(keep, within + slot_of * residues, -1)
        rows = []
        for k in range(neighbour_count):
            place_k = jnp.broadcast_to(place[:, k : k + 1], (rows_at_once, LANES))
            place_k = place_k.astype(jnp.int16)
            parts = [
                jnp.where(place_k == lane_short + jnp.int16(slot * residues), one, zero)
                for slot in range(3)
            ]
            distance_k = jnp.broadcast_to(distance[:, k : k + 1], (rows_at_once, LANES))
            scaled = (distance_k - centres) * (1.0 / 1.25)
            radial = jnp.where(lane < bins, jnp.exp(-scaled * scaled), 0.0)
            parts.append(radial.astype(BF16))
            rows.append(jnp.concatenate(parts, axis=1))
        selector = jnp.concatenate(rows, axis=0)
        width = 256
        for column in range(feature_dim // width):
            cols = slice(column * width, (column + 1) * width)
            preact = jnp.dot(selector, window_ref[:, cols], preferred_element_type=F32)
            doubled = preact * (1.0 + lax.erf(preact * (0.5**0.5)))
            message_ref[pl.ds(begin, rows_at_once), cols] = jnp.sum(
                doubled.reshape(neighbour_count, rows_at_once, width), axis=0
            ) * (0.5 / 30.0)

    for copy in copies[len(early) :]:
        copy.wait()
    values = feats_buf[first_row : first_row + count, :].astype(F32) + message_ref[...]
    centred = values - jnp.mean(values, axis=1, keepdims=True)
    spread = jnp.mean(centred * centred, axis=1, keepdims=True)
    mixed = (centred * lax.rsqrt(spread + 1e-5) * gain_buf[...]).astype(BF16)
    half = LANES // 2
    w_logit = jnp.concatenate(
        [w_logit_buf[...].astype(F32), jnp.zeros((LANES - vocab_size, feature_dim), F32)], axis=0
    ).astype(BF16)
    logits = lax.dot_general(
        mixed, w_logit, (((1,), (1,)), ((), ())), preferred_element_type=F32
    )
    bounded = 8.0 * jnp.tanh(logits * 0.125)
    token = lax.broadcasted_iota(jnp.int32, logits.shape, 1)
    exponent = jnp.where(token < vocab_size, jnp.exp(bounded), 0.0)
    probability = (exponent / jnp.sum(exponent, axis=1, keepdims=True)).astype(BF16)
    residue = (
        block_index * residues + first_row + lax.broadcasted_iota(jnp.int32, (count, 1), 0)
    )
    valid = (residue < residue_count).astype(F32)
    table = jnp.concatenate(
        [
            table_buf[...].astype(F32),
            jnp.zeros((LANES - vocab_size, table_buf.shape[1]), F32),
        ],
        axis=0,
    ).astype(BF16)
    soft = (jnp.dot(probability, table, preferred_element_type=F32) * valid).astype(BF16)
    shown_ref[...] = (probability.astype(F32) * valid).astype(BF16)
    soft_wide = soft.astype(F32)
    soft_centred = soft_wide - jnp.mean(soft_wide, axis=1, keepdims=True)
    soft_spread = jnp.mean(soft_centred * soft_centred, axis=1, keepdims=True)
    coded = probability.astype(F32) * (lax.rsqrt(soft_spread + 1e-5) * valid)
    high, low = high_low(coded)
    coded_ref[...] = jnp.concatenate([high[:, :half], low[:, :half]], axis=1)
    if tokens:
        wide = table.astype(F32)[:half]
        wide = wide - jnp.mean(wide, axis=1, keepdims=True)
        scaled_ref[...] = (wide * token_gain_buf[...]).astype(BF16)
        depth = w_up_buf.shape[0]
        part = scaled_ref[:, pl.ds(pl.multiple_of(scalar_ref[2] * depth, LANES), depth)]
        token_ref[...] = jnp.dot(part, w_up_buf[...], preferred_element_type=F32)


def messages(own, side, other, feats, links, w_rbf, gain, w_logit, table, scalars, rows, tokens):
    residues, feature_dim = feats.shape
    embed_dim = table.shape[1]
    bins = w_rbf.shape[0]
    depth = -(-(3 * residues + bins) // 256) * 256
    count = rows[1] - rows[0]
    in_vmem = pl.BlockSpec(memory_space=pltpu.VMEM)
    in_hbm_spec = pl.BlockSpec(memory_space=pltpu.HBM)
    arrays = [own, side, other, feats, links, w_rbf, gain, w_logit, table, *tokens]
    out_shape = [jax.ShapeDtypeStruct((count, LANES), BF16)] * 2
    scratch = [
        pltpu.VMEM((depth, feature_dim), BF16),
        pltpu.VMEM((3, COORD_ROWS, residues), BF16),
        pltpu.VMEM(feats.shape, BF16),
        pltpu.VMEM(links.shape, jnp.int32),
        pltpu.VMEM(gain.shape, F32),
        pltpu.VMEM(w_logit.shape, BF16),
        pltpu.VMEM(table.shape, BF16),
        pltpu.VMEM((residues, LANES), jnp.int32),
        pltpu.VMEM((residues, LANES), F32),
        pltpu.VMEM((count, feature_dim), F32),
        pltpu.SemaphoreType.DMA((16,)),
    ]
    if tokens:
        token_gain, w_up = tokens
        out_shape.append(jax.ShapeDtypeStruct((LANES // 2, w_up.shape[1]), F32))
        scratch += [
            pltpu.VMEM(token_gain.shape, F32),
            pltpu.VMEM(w_up.shape, BF16),
            pltpu.VMEM((LANES // 2, embed_dim), BF16),
        ]
    return pl.pallas_call(
        functools.partial(message_kernel, min(32, count), rows[0], bool(tokens)),
        out_shape=out_shape,
        in_specs=[in_hbm_spec] * len(arrays) + [pl.BlockSpec(memory_space=pltpu.SMEM)],
        out_specs=[in_vmem] * len(out_shape),
        scratch_shapes=scratch,
        compiler_params=pltpu.CompilerParams(vmem_limit_bytes=20 << 20),
        cost_estimate=pl.CostEstimate(
            flops=100_000_000 * count, bytes_accessed=5_000_000, transcendentals=50_000 * count
        ),
        name="messages",
    )(*in_hbm(*arrays), scalars)


def gelu_rows(rows, up):
    total = jnp.dot(rows, jnp.concatenate([up, up], axis=0), preferred_element_type=F32)
    return (0.5 * total * (1.0 + lax.erf(total * (0.5**0.5)))).astype(BF16)


def trunk_kernel(blocks, columns, targets, table_columns, *refs):
    coded, up_ref, refs = refs[:blocks], refs[blocks], refs[blocks + 1 :]
    weights, refs = refs[: len(columns)], refs[len(columns) :]
    if table_columns:
        shown_ref, turn_ref, table_ref, refs = refs[0], refs[1], refs[2], refs[3:]
        refs, (table_raw, table_buf, base_buf, extra) = refs[:-4], refs[-4:]
        base_ref, refs = refs[0], refs[1:]
        fetching = pltpu.make_async_copy(table_ref, table_raw, extra.at[0])
        fetching.start()
    outs = refs[:-5]
    buffer, inner, results, arrived, left = refs[-5:]
    chunk = buffer.shape[2]
    copies = [
        pltpu.make_async_copy(
            ref.at[:, first : first + chunk], buffer.at[place], arrived.at[place]
        )
        for place, (ref, first) in enumerate(zip(weights, columns))
    ]
    for copy in copies:
        copy.start()
    rows = coded[0].shape[0]
    for place, ref in enumerate(coded):
        inner[place * rows : (place + 1) * rows, :] = gelu_rows(ref[...], up_ref[...])
    leaving = []
    for place, copy in enumerate(copies):
        copy.wait()
        value = jnp.dot(inner[...], buffer[place], preferred_element_type=F32)
        if table_columns:
            if place == 0:
                fetching.wait()
                filler = (table_buf.shape[0] - table_raw.shape[0], table_raw.shape[1])
                table_buf[...] = jnp.concatenate(
                    [table_raw[...].astype(F32), jnp.zeros(filler, F32)], axis=0
                ).astype(BF16)
            half_width = table_buf.shape[1] // 2
            first = pl.multiple_of(
                lax.rem(turn_ref[0] * half_width + table_columns[place], 2 * half_width), LANES
            )
            soft = jnp.dot(
                shown_ref[...], table_buf[:, pl.ds(first, chunk)], preferred_element_type=F32
            )
            base_buf[:, place * chunk : (place + 1) * chunk] = value[
                (blocks - 1) * rows :
            ].astype(BF16).astype(F32) + soft.astype(BF16).astype(F32)
            value = value[: (blocks - 1) * rows]
        results[place] = value.astype(BF16)
        for number, (start, stop) in enumerate(targets):
            leaving.append(
                pltpu.make_async_copy(
                    results.at[place, start:stop, :],
                    outs[number].at[:, place * chunk : (place + 1) * chunk],
                    left.at[len(leaving)],
                )
            )
            leaving[-1].start()
    if table_columns:
        leaving.append(pltpu.make_async_copy(base_buf, base_ref, extra.at[1]))
        leaving[-1].start()
    for copy in leaving:
        copy.wait()


def trunk(coded, up, pieces, targets, chunk, shown=None, turn=None, table=None):
    with_base = table is not None
    kept = len(coded) - with_base
    rows, hidden = coded[0].shape[0], up.shape[1]
    in_vmem = pl.BlockSpec(memory_space=pltpu.VMEM)
    hbm_spec = pl.BlockSpec(memory_space=pltpu.HBM)
    return pl.pallas_call(
        functools.partial(
            trunk_kernel,
            len(coded),
            [column for _, column in pieces],
            targets,
            [place * chunk for place in range(len(pieces))] if with_base else (),
        ),
        out_shape=[pltpu.HBM((rows, len(pieces) * chunk), F32)] * with_base
        + [pltpu.HBM((stop - start, len(pieces) * chunk), BF16) for start, stop in targets],
        in_specs=[in_vmem] * (len(coded) + 1) + [pl.BlockSpec(memory_space=pl.ANY)] * len(pieces)
        + [in_vmem, pl.BlockSpec(memory_space=pltpu.SMEM), hbm_spec] * with_base,
        out_specs=[hbm_spec] * (with_base + len(targets)),
        scratch_shapes=[
            pltpu.VMEM((len(pieces), hidden, chunk), BF16),
            pltpu.VMEM((len(coded) * rows, hidden), BF16),
            pltpu.VMEM((len(pieces), kept * rows, chunk), BF16),
            pltpu.SemaphoreType.DMA((len(pieces),)),
            pltpu.SemaphoreType.DMA((len(pieces) * len(targets),)),
        ]
        + (
            [
                pltpu.VMEM(table.shape, BF16),
                pltpu.VMEM((LANES, table.shape[1]), BF16),
                pltpu.VMEM((rows, len(pieces) * chunk), F32),
                pltpu.SemaphoreType.DMA((2,)),
            ]
            if with_base
            else []
        ),
        compiler_params=pltpu.CompilerParams(vmem_limit_bytes=16 << 20),
        cost_estimate=pl.CostEstimate(
            flops=2 * len(coded) * rows * len(pieces) * hidden * chunk,
            bytes_accessed=2 * hidden * chunk * len(pieces),
            transcendentals=len(coded) * rows * hidden,
        ),
        name="trunk",
    )(
        *coded,
        up,
        *[array for array, _ in pieces],
        *((shown, turn, in_hbm(table)[0]) if with_base else ()),
    )


def rounded_sum(left, right):
    return (left.astype(F32) + right.astype(F32)).astype(BF16)


def on_device(
    node_feats,
    coords,
    neighbours,
    counts,
    w_near,
    w_rbf,
    gen_gain,
    w_logit,
    embed_table,
    trunk_gain,
    w_up,
    w_down,
):
    backbones, residues, feature_dim = node_feats.shape
    assert backbones == 1 and lax.axis_size("mp") == 4
    vocab_size, embed_dim = embed_table.shape
    half = LANES // 2
    seq_count = lax.axis_size("seq")
    seq_index = lax.axis_index("seq")
    block_index = lax.axis_index("mp")

    own = near_rows(node_feats[0], coords[0], w_near)
    side = swap(own, "mp", 1)
    other = lax.ppermute(own, "mp", [(1, 2), (2, 1)])

    scalars = jnp.stack([block_index.astype(jnp.int32), counts[0], seq_index.astype(jnp.int32)])

    in_kernel = seq_count == 2 and w_up.shape[0] % LANES == 0
    shown, coded, *token_up = messages(
        own,
        side,
        other,
        node_feats[0],
        neighbours[0].T,
        w_rbf,
        gen_gain[None, :],
        w_logit.T,
        embed_table,
        scalars,
        (0, residues),
        (trunk_gain[None, :], w_up) if in_kernel else (),
    )
    if in_kernel:
        token_up = (token_up[0] + swap(token_up[0], "seq", 1)).astype(BF16)
        whole = in_hbm(w_down) + [swap(w_down, "seq", 1)]
    else:
        table_wide = embed_table.astype(F32)
        table_centred = table_wide - jnp.mean(table_wide, axis=1, keepdims=True)
        table_scaled = jnp.pad(
            (table_centred * trunk_gain).astype(BF16), ((0, half - vocab_size), (0, 0))
        )
        table_part = lax.dynamic_slice_in_dim(
            table_scaled, seq_index * w_up.shape[0], w_up.shape[0], 1
        )
        token_up = lax.psum(
            jnp.dot(table_part, w_up, preferred_element_type=F32), "seq"
        ).astype(BF16)
        whole = [lax.all_gather(w_down, "seq", axis=1, tiled=True)]
    chunk = embed_dim // 4
    pieces = [(part, first) for part in whole for first in range(0, part.shape[1], chunk)]

    inward = [(0, 1), (3, 2)]
    crossing = [(1, 2), (2, 1)]
    skipping = [(1, 3), (2, 0)]
    coded_3, coded_2, coded_1 = [swap(coded, "mp", step) for step in (3, 2, 1)]
    coded_3, coded_2, coded_1, token_up = lax.optimization_barrier(
        (coded_3, coded_2, coded_1, token_up)
    )
    pairs = [(0, 2 * residues)]
    (far_a,) = trunk([coded_3, coded_2], token_up, pieces[:2], pairs, chunk)
    coded_1, _ = lax.optimization_barrier((coded_1, far_a))
    turn = seq_index.astype(jnp.int32) if len(whole) == 2 else jnp.zeros((), jnp.int32)
    base, near = trunk(
        [coded_1, coded],
        token_up,
        pieces,
        [(0, residues)],
        chunk,
        shown,
        turn[None],
        embed_table,
    )
    coded_3, _ = lax.optimization_barrier((coded_3, near))
    (far_b,) = trunk([coded_3, coded_2], token_up, pieces[2:], pairs, chunk)
    arrived_a = lax.ppermute(far_a, "mp", inward)
    to_edge = lax.ppermute(near, "mp", [(1, 0), (2, 3)])
    arrived_b = lax.ppermute(far_b, "mp", inward)
    arrived_a, far_a, _ = lax.optimization_barrier((arrived_a, far_a, far_b))
    near, _ = lax.optimization_barrier((near, arrived_b))
    to_inner = lax.ppermute(near, "mp", inward)
    sums = []
    for far, arrived in ((far_a, arrived_a), (far_b, arrived_b)):
        across = rounded_sum(far[:residues], arrived[residues:])
        beyond = rounded_sum(far[residues:], arrived[:residues])
        across = lax.ppermute(across, "mp", crossing)
        beyond = lax.ppermute(beyond, "mp", skipping)
        sums.append(across.astype(F32) + beyond.astype(F32))
    total = base + to_edge.astype(F32) + to_inner.astype(F32)
    total = total + jnp.concatenate(sums, axis=1)
    if len(whole) == 2:
        middle = embed_dim // 2
        turned = jnp.concatenate([total[:, middle:], total[:, :middle]], axis=1)
        total = jnp.where(seq_index == 0, total, turned)
    return total.astype(BF16)[None]


def solution(mesh):
    placed = (
        P(("dp", "seq"), "mp", None),
        P(("dp", "seq"), None, "mp"),
        P(("dp", "seq"), "mp", None),
        P(("dp", "seq")),
        P(),
        P(),
        P(),
        P(),
        P(),
        P(),
        P("seq", "mp"),
        P("mp", "seq"),
    )
    return jax.shard_map(
        on_device,
        mesh=mesh,
        in_specs=placed,
        out_specs=P(("dp", "seq"), "mp", None),
        check_vma=False,
    )
```

```python
import functools

import jax
import jax.numpy as jnp
from jax import lax
from jax.experimental import pallas as pl
from jax.experimental.pallas import tpu as pltpu
from jax.sharding import PartitionSpec as P

F32 = jnp.float32
BF16 = jnp.bfloat16
LANES = 128
COORD_ROWS = 16


def swap(value, axis, step):
    count = lax.axis_size(axis)
    return lax.ppermute(value, axis, [(i, i ^ step) for i in range(count)])


def high_low(value):
    high = value.astype(BF16)
    low = (value - high.astype(F32)).astype(BF16)
    return high, low


def in_hbm(*arrays):
    return [pltpu.with_memory_space_constraint(array, pltpu.HBM) for array in arrays]


def near_kernel(feats_ref, xyz_ref, w_near_ref, out_ref, feats, xyz, weights, arrived):
    residues = feats.shape[0]
    parts, height, depth = weights.shape
    copies = [
        pltpu.make_async_copy(feats_ref, feats, arrived.at[parts]),
        pltpu.make_async_copy(xyz_ref, xyz, arrived.at[parts + 1]),
    ] + [
        pltpu.make_async_copy(
            w_near_ref.at[part * height : (part + 1) * height, :],
            weights.at[part],
            arrived.at[part],
        )
        for part in range(parts)
    ]
    for copy in copies:
        copy.start()
    out_ref[residues:, :] = jnp.zeros((COORD_ROWS, depth), BF16)
    copies[0].wait()
    copies[1].wait()
    out_ref[residues : residues + 3, 0:residues] = xyz[...]
    near = None
    for part in range(parts):
        copies[2 + part].wait()
        term = jnp.dot(
            feats[:, part * height : (part + 1) * height],
            weights[part],
            preferred_element_type=F32,
        )
        near = term if near is None else near + term
    out_ref[0:residues, :] = near.astype(BF16)


def near_rows(feats, xyz, w_near):
    residues, depth = feats.shape
    parts = 4
    return pl.pallas_call(
        near_kernel,
        out_shape=jax.ShapeDtypeStruct((residues + COORD_ROWS, depth), BF16),
        in_specs=[pl.BlockSpec(memory_space=pltpu.HBM)] * 3,
        out_specs=pl.BlockSpec(memory_space=pltpu.VMEM),
        scratch_shapes=[
            pltpu.VMEM(feats.shape, BF16),
            pltpu.VMEM(xyz.shape, BF16),
            pltpu.VMEM((parts, depth // parts, depth), BF16),
            pltpu.SemaphoreType.DMA((parts + 2,)),
        ],
        name="near_rows",
    )(*in_hbm(feats, xyz, w_near))


def token_kernel(turn_ref, table_ref, gain_ref, w_up_ref, out_ref, scaled_ref):
    wide = table_ref[...].astype(F32)
    wide = wide - jnp.mean(wide, axis=1, keepdims=True)
    scaled = wide * gain_ref[...]
    filler = jnp.zeros((scaled_ref.shape[0] - scaled.shape[0], scaled.shape[1]), F32)
    scaled_ref[...] = jnp.concatenate([scaled, filler], axis=0).astype(BF16)
    depth = w_up_ref.shape[0]
    part = scaled_ref[:, pl.ds(pl.multiple_of(turn_ref[0] * depth, LANES), depth)]
    out_ref[...] = jnp.dot(part, w_up_ref[...], preferred_element_type=F32)


def token_rows(turn, table, gain, w_up):
    in_vmem = pl.BlockSpec(memory_space=pltpu.VMEM)
    return pl.pallas_call(
        token_kernel,
        out_shape=jax.ShapeDtypeStruct((LANES // 2, w_up.shape[1]), F32),
        in_specs=[pl.BlockSpec(memory_space=pltpu.SMEM)] + [in_vmem] * 3,
        out_specs=in_vmem,
        scratch_shapes=[pltpu.VMEM((LANES // 2, table.shape[1]), BF16)],
        name="token_rows",
    )(turn, table, gain, w_up)


def message_kernel(
    rows_at_once,
    first_row,
    with_tokens,
    *refs,
):
    if with_tokens:
        (token_gain_ref, w_up_ref), refs = refs[9:11], refs[:9] + refs[11:]
        (token_ref,), refs = refs[12:13], refs[:12] + refs[13:]
        (token_gain_buf, w_up_buf, scaled_ref), refs = refs[-3:], refs[:-3]
    message_body(
        rows_at_once,
        first_row,
        (token_gain_ref, w_up_ref, token_ref, token_gain_buf, w_up_buf, scaled_ref)
        if with_tokens
        else None,
        *refs,
    )


def message_body(
    rows_at_once,
    first_row,
    tokens,
    own_ref,
    side_ref,
    other_ref,
    feats_ref,
    link_ref,
    w_rbf_ref,
    gain_ref,
    w_logit_ref,
    table_ref,
    scalar_ref,
    shown_ref,
    coded_ref,
    window_ref,
    position_ref,
    feats_buf,
    link_buf,
    gain_buf,
    w_logit_buf,
    table_buf,
    place_ref,
    xyz_ref,
    message_ref,
    arrived,
):
    neighbour_count, residues = link_ref.shape
    bins, feature_dim = w_rbf_ref.shape
    vocab_size = table_ref.shape[0]
    window = 3 * residues
    early = []
    for slot, ref in enumerate((own_ref, side_ref, other_ref)):
        early.append(
            (ref.at[0:residues, :], window_ref.at[slot * residues : (slot + 1) * residues, :])
        )
        early.append(
            (ref.at[residues : residues + COORD_ROWS, 0:residues], position_ref.at[slot])
        )
    early.append((w_rbf_ref, window_ref.at[window : window + bins, :]))
    early.append((link_ref, link_buf))
    late = [
        (feats_ref, feats_buf),
        (gain_ref, gain_buf),
        (w_logit_ref, w_logit_buf),
        (table_ref, table_buf),
    ]
    if tokens:
        token_gain_ref, w_up_ref, token_ref, token_gain_buf, w_up_buf, scaled_ref = tokens
        late += [(token_gain_ref, token_gain_buf), (w_up_ref, w_up_buf)]
    copies = [
        pltpu.make_async_copy(source, target, arrived.at[place])
        for place, (source, target) in enumerate(early + late)
    ]
    for copy in copies:
        copy.start()
    window_ref[window + bins :, :] = jnp.zeros(
        (window_ref.shape[0] - window - bins, feature_dim), BF16
    )
    for copy in copies[: len(early)]:
        copy.wait()

    block_index = scalar_ref[0]
    residue_count = scalar_ref[1]
    positions = [position_ref[slot].astype(F32) for slot in range(3)]
    xyz_ref[...] = jnp.transpose(
        jnp.concatenate([positions[0], jnp.zeros((LANES - COORD_ROWS, residues), F32)], axis=0)
    )
    place_ref[...] = jnp.transpose(
        jnp.concatenate(
            [link_buf[...], jnp.zeros((LANES - neighbour_count, residues), jnp.int32)], axis=0
        )
    )
    lane = lax.broadcasted_iota(jnp.int32, (rows_at_once, LANES), 1)
    centres = 2.0 + (20.0 / (bins - 1)) * lane.astype(F32)

    lane_short = lane.astype(jnp.int16)
    one, zero = jnp.ones((), BF16), jnp.zeros((), BF16)
    count = message_ref.shape[0]
    for begin in range(0, count, rows_at_once):
        first = first_row + begin
        links = place_ref[pl.ds(first, rows_at_once), :]
        keep = (links < residue_count) & (lane < neighbour_count)
        within = jnp.bitwise_and(links, residues - 1)
        block_of = lax.shift_right_logical(links, residues.bit_length() - 1)
        side_block = jnp.bitwise_xor(block_index, 1)
        slot_of = jnp.where(
            block_of == block_index, 0, jnp.where(block_of == side_block, 1, 2)
        )
        own_xyz = xyz_ref[pl.ds(first, rows_at_once), :]
        squared = None
        for slot in range(3):
            total = None
            for axis in range(3):
                offset = own_xyz[:, axis : axis + 1] - positions[slot][axis : axis + 1, :]
                total = offset * offset if total is None else total + offset * offset
            picked = jnp.take_along_axis(total, within, axis=1)
            squared = picked if squared is None else jnp.where(slot_of == slot, picked, squared)
        distance = jnp.where(keep, jnp.sqrt(squared), 1e6)
        place = jnp.where(keep, within + slot_of * residues, -1)
        rows = []
        for k in range(neighbour_count):
            place_k = jnp.broadcast_to(place[:, k : k + 1], (rows_at_once, LANES))
            place_k = place_k.astype(jnp.int16)
            parts = [
                jnp.where(place_k == lane_short + jnp.int16(slot * residues), one, zero)
                for slot in range(3)
            ]
            distance_k = jnp.broadcast_to(distance[:, k : k + 1], (rows_at_once, LANES))
            scaled = (distance_k - centres) * (1.0 / 1.25)
            radial = jnp.where(lane < bins, jnp.exp(-scaled * scaled), 0.0)
            parts.append(radial.astype(BF16))
            rows.append(jnp.concatenate(parts, axis=1))
        selector = jnp.concatenate(rows, axis=0)
        width = 256
        for column in range(feature_dim // width):
            cols = slice(column * width, (column + 1) * width)
            preact = jnp.dot(selector, window_ref[:, cols], preferred_element_type=F32)
            doubled = preact * (1.0 + lax.erf(preact * (0.5**0.5)))
            message_ref[pl.ds(begin, rows_at_once), cols] = jnp.sum(
                doubled.reshape(neighbour_count, rows_at_once, width), axis=0
            ) * (0.5 / 30.0)

    for copy in copies[len(early) :]:
        copy.wait()
    values = feats_buf[first_row : first_row + count, :].astype(F32) + message_ref[...]
    centred = values - jnp.mean(values, axis=1, keepdims=True)
    spread = jnp.mean(centred * centred, axis=1, keepdims=True)
    mixed = (centred * lax.rsqrt(spread + 1e-5) * gain_buf[...]).astype(BF16)
    half = LANES // 2
    w_logit = jnp.concatenate(
        [w_logit_buf[...].astype(F32), jnp.zeros((LANES - vocab_size, feature_dim), F32)], axis=0
    ).astype(BF16)
    logits = lax.dot_general(
        mixed, w_logit, (((1,), (1,)), ((), ())), preferred_element_type=F32
    )
    bounded = 8.0 * jnp.tanh(logits * 0.125)
    token = lax.broadcasted_iota(jnp.int32, logits.shape, 1)
    exponent = jnp.where(token < vocab_size, jnp.exp(bounded), 0.0)
    probability = (exponent / jnp.sum(exponent, axis=1, keepdims=True)).astype(BF16)
    residue = (
        block_index * residues + first_row + lax.broadcasted_iota(jnp.int32, (count, 1), 0)
    )
    valid = (residue < residue_count).astype(F32)
    table = jnp.concatenate(
        [
            table_buf[...].astype(F32),
            jnp.zeros((LANES - vocab_size, table_buf.shape[1]), F32),
        ],
        axis=0,
    ).astype(BF16)
    soft = (jnp.dot(probability, table, preferred_element_type=F32) * valid).astype(BF16)
    shown_ref[...] = (probability.astype(F32) * valid).astype(BF16)
    soft_wide = soft.astype(F32)
    soft_centred = soft_wide - jnp.mean(soft_wide, axis=1, keepdims=True)
    soft_spread = jnp.mean(soft_centred * soft_centred, axis=1, keepdims=True)
    coded = probability.astype(F32) * (lax.rsqrt(soft_spread + 1e-5) * valid)
    high, low = high_low(coded)
    coded_ref[...] = jnp.concatenate([high[:, :half], low[:, :half]], axis=1)
    if tokens:
        wide = table.astype(F32)[:half]
        wide = wide - jnp.mean(wide, axis=1, keepdims=True)
        scaled_ref[...] = (wide * token_gain_buf[...]).astype(BF16)
        depth = w_up_buf.shape[0]
        part = scaled_ref[:, pl.ds(pl.multiple_of(scalar_ref[2] * depth, LANES), depth)]
        token_ref[...] = jnp.dot(part, w_up_buf[...], preferred_element_type=F32)


def messages(own, side, other, feats, links, w_rbf, gain, w_logit, table, scalars, rows, tokens):
    residues, feature_dim = feats.shape
    embed_dim = table.shape[1]
    bins = w_rbf.shape[0]
    depth = -(-(3 * residues + bins) // 256) * 256
    count = rows[1] - rows[0]
    in_vmem = pl.BlockSpec(memory_space=pltpu.VMEM)
    in_hbm_spec = pl.BlockSpec(memory_space=pltpu.HBM)
    arrays = [own, side, other, feats, links, w_rbf, gain, w_logit, table, *tokens]
    out_shape = [jax.ShapeDtypeStruct((count, LANES), BF16)] * 2
    scratch = [
        pltpu.VMEM((depth, feature_dim), BF16),
        pltpu.VMEM((3, COORD_ROWS, residues), BF16),
        pltpu.VMEM(feats.shape, BF16),
        pltpu.VMEM(links.shape, jnp.int32),
        pltpu.VMEM(gain.shape, F32),
        pltpu.VMEM(w_logit.shape, BF16),
        pltpu.VMEM(table.shape, BF16),
        pltpu.VMEM((residues, LANES), jnp.int32),
        pltpu.VMEM((residues, LANES), F32),
        pltpu.VMEM((count, feature_dim), F32),
        pltpu.SemaphoreType.DMA((16,)),
    ]
    if tokens:
        token_gain, w_up = tokens
        out_shape.append(jax.ShapeDtypeStruct((LANES // 2, w_up.shape[1]), F32))
        scratch += [
            pltpu.VMEM(token_gain.shape, F32),
            pltpu.VMEM(w_up.shape, BF16),
            pltpu.VMEM((LANES // 2, embed_dim), BF16),
        ]
    return pl.pallas_call(
        functools.partial(message_kernel, min(32, count), rows[0], bool(tokens)),
        out_shape=out_shape,
        in_specs=[in_hbm_spec] * len(arrays) + [pl.BlockSpec(memory_space=pltpu.SMEM)],
        out_specs=[in_vmem] * len(out_shape),
        scratch_shapes=scratch,
        compiler_params=pltpu.CompilerParams(vmem_limit_bytes=20 << 20),
        cost_estimate=pl.CostEstimate(
            flops=100_000_000 * count, bytes_accessed=5_000_000, transcendentals=50_000 * count
        ),
        name="messages",
    )(*in_hbm(*arrays), scalars)


def gelu_rows(rows, up):
    total = jnp.dot(rows, jnp.concatenate([up, up], axis=0), preferred_element_type=F32)
    return (0.5 * total * (1.0 + lax.erf(total * (0.5**0.5)))).astype(BF16)


def trunk_kernel(blocks, columns, targets, table_columns, *refs):
    coded, up_ref, refs = refs[:blocks], refs[blocks], refs[blocks + 1 :]
    weights, refs = refs[: len(columns)], refs[len(columns) :]
    if table_columns:
        shown_ref, turn_ref, table_ref, refs = refs[0], refs[1], refs[2], refs[3:]
        refs, (table_raw, table_buf, base_buf, extra) = refs[:-4], refs[-4:]
        base_ref, refs = refs[0], refs[1:]
        fetching = pltpu.make_async_copy(table_ref, table_raw, extra.at[0])
        fetching.start()
    outs = refs[:-3]
    inner, results, left = refs[-3:]
    chunk = results.shape[2]
    rows = coded[0].shape[0]
    for place, ref in enumerate(coded):
        inner[place * rows : (place + 1) * rows, :] = gelu_rows(ref[...], up_ref[...])
    leaving = []
    for place, (ref, first) in enumerate(zip(weights, columns)):
        value = jnp.dot(
            inner[...], ref[:, first : first + chunk], preferred_element_type=F32
        )
        if table_columns:
            if place == 0:
                fetching.wait()
                filler = (table_buf.shape[0] - table_raw.shape[0], table_raw.shape[1])
                table_buf[...] = jnp.concatenate(
                    [table_raw[...].astype(F32), jnp.zeros(filler, F32)], axis=0
                ).astype(BF16)
            half_width = table_buf.shape[1] // 2
            first = pl.multiple_of(
                lax.rem(turn_ref[0] * half_width + table_columns[place], 2 * half_width), LANES
            )
            soft = jnp.dot(
                shown_ref[...], table_buf[:, pl.ds(first, chunk)], preferred_element_type=F32
            )
            base_buf[:, place * chunk : (place + 1) * chunk] = value[
                (blocks - 1) * rows :
            ].astype(BF16).astype(F32) + soft.astype(BF16).astype(F32)
            value = value[: (blocks - 1) * rows]
        results[place] = value.astype(BF16)
        for number, (start, stop) in enumerate(targets):
            leaving.append(
                pltpu.make_async_copy(
                    results.at[place, start:stop, :],
                    outs[number].at[:, place * chunk : (place + 1) * chunk],
                    left.at[len(leaving)],
                )
            )
            leaving[-1].start()
    if table_columns:
        leaving.append(pltpu.make_async_copy(base_buf, base_ref, extra.at[1]))
        leaving[-1].start()
    for copy in leaving:
        copy.wait()


def trunk(coded, up, pieces, targets, chunk, shown=None, turn=None, table=None):
    with_base = table is not None
    kept = len(coded) - with_base
    rows, hidden = coded[0].shape[0], up.shape[1]
    in_vmem = pl.BlockSpec(memory_space=pltpu.VMEM)
    hbm_spec = pl.BlockSpec(memory_space=pltpu.HBM)
    return pl.pallas_call(
        functools.partial(
            trunk_kernel,
            len(coded),
            [column for _, column in pieces],
            targets,
            [place * chunk for place in range(len(pieces))] if with_base else (),
        ),
        out_shape=[pltpu.HBM((rows, len(pieces) * chunk), F32)] * with_base
        + [pltpu.HBM((stop - start, len(pieces) * chunk), BF16) for start, stop in targets],
        in_specs=[in_vmem] * (len(coded) + 1) + [in_vmem] * len(pieces)
        + [in_vmem, pl.BlockSpec(memory_space=pltpu.SMEM), hbm_spec] * with_base,
        out_specs=[hbm_spec] * (with_base + len(targets)),
        scratch_shapes=[
            pltpu.VMEM((len(coded) * rows, hidden), BF16),
            pltpu.VMEM((len(pieces), kept * rows, chunk), BF16),
            pltpu.SemaphoreType.DMA((len(pieces) * len(targets),)),
        ]
        + (
            [
                pltpu.VMEM(table.shape, BF16),
                pltpu.VMEM((LANES, table.shape[1]), BF16),
                pltpu.VMEM((rows, len(pieces) * chunk), F32),
                pltpu.SemaphoreType.DMA((2,)),
            ]
            if with_base
            else []
        ),
        compiler_params=pltpu.CompilerParams(vmem_limit_bytes=16 << 20),
        cost_estimate=pl.CostEstimate(
            flops=2 * len(coded) * rows * len(pieces) * hidden * chunk,
            bytes_accessed=2 * hidden * chunk * len(pieces),
            transcendentals=len(coded) * rows * hidden,
        ),
        name="trunk",
    )(
        *coded,
        up,
        *[array for array, _ in pieces],
        *((shown, turn, in_hbm(table)[0]) if with_base else ()),
    )


def rounded_sum(left, right):
    return (left.astype(F32) + right.astype(F32)).astype(BF16)


def on_device(
    node_feats,
    coords,
    neighbours,
    counts,
    w_near,
    w_rbf,
    gen_gain,
    w_logit,
    embed_table,
    trunk_gain,
    w_up,
    w_down,
):
    backbones, residues, feature_dim = node_feats.shape
    assert backbones == 1 and lax.axis_size("mp") == 4
    vocab_size, embed_dim = embed_table.shape
    half = LANES // 2
    seq_count = lax.axis_size("seq")
    seq_index = lax.axis_index("seq")
    block_index = lax.axis_index("mp")

    own = near_rows(node_feats[0], coords[0], w_near)
    side = swap(own, "mp", 1)
    other = lax.ppermute(own, "mp", [(1, 2), (2, 1)])

    scalars = jnp.stack([block_index.astype(jnp.int32), counts[0], seq_index.astype(jnp.int32)])

    in_kernel = seq_count == 2 and w_up.shape[0] % LANES == 0
    if in_kernel:
        token_up = token_rows(
            seq_index.astype(jnp.int32)[None], embed_table, trunk_gain[None, :], w_up
        )
        token_up = (token_up + swap(token_up, "seq", 1)).astype(BF16)
    shown, coded = messages(
        own,
        side,
        other,
        node_feats[0],
        neighbours[0].T,
        w_rbf,
        gen_gain[None, :],
        w_logit.T,
        embed_table,
        scalars,
        (0, residues),
        (),
    )
    if in_kernel:
        whole = [w_down] + [swap(w_down, "seq", 1)]
    else:
        table_wide = embed_table.astype(F32)
        table_centred = table_wide - jnp.mean(table_wide, axis=1, keepdims=True)
        table_scaled = jnp.pad(
            (table_centred * trunk_gain).astype(BF16), ((0, half - vocab_size), (0, 0))
        )
        table_part = lax.dynamic_slice_in_dim(
            table_scaled, seq_index * w_up.shape[0], w_up.shape[0], 1
        )
        token_up = lax.psum(
            jnp.dot(table_part, w_up, preferred_element_type=F32), "seq"
        ).astype(BF16)
        whole = [lax.all_gather(w_down, "seq", axis=1, tiled=True)]
    chunk = embed_dim // 4
    pieces = [(part, first) for part in whole for first in range(0, part.shape[1], chunk)]

    inward = [(0, 1), (3, 2)]
    crossing = [(1, 2), (2, 1)]
    skipping = [(1, 3), (2, 0)]
    coded_3, coded_2, coded_1 = [swap(coded, "mp", step) for step in (3, 2, 1)]
    coded_3, coded_2, coded_1, token_up = lax.optimization_barrier(
        (coded_3, coded_2, coded_1, token_up)
    )
    pairs = [(0, 2 * residues)]
    (far_a,) = trunk([coded_3, coded_2], token_up, pieces[:2], pairs, chunk)
    coded_1, _ = lax.optimization_barrier((coded_1, far_a))
    turn = seq_index.astype(jnp.int32) if len(whole) == 2 else jnp.zeros((), jnp.int32)
    base, near = trunk(
        [coded_1, coded],
        token_up,
        pieces,
        [(0, residues)],
        chunk,
        shown,
        turn[None],
        embed_table,
    )
    coded_3, _ = lax.optimization_barrier((coded_3, near))
    (far_b,) = trunk([coded_3, coded_2], token_up, pieces[2:], pairs, chunk)
    arrived_a = lax.ppermute(far_a, "mp", inward)
    to_edge = lax.ppermute(near, "mp", [(1, 0), (2, 3)])
    arrived_b = lax.ppermute(far_b, "mp", inward)
    arrived_a, far_a, _ = lax.optimization_barrier((arrived_a, far_a, far_b))
    near, _ = lax.optimization_barrier((near, arrived_b))
    to_inner = lax.ppermute(near, "mp", inward)
    sums = []
    for far, arrived in ((far_a, arrived_a), (far_b, arrived_b)):
        across = rounded_sum(far[:residues], arrived[residues:])
        beyond = rounded_sum(far[residues:], arrived[:residues])
        across = lax.ppermute(across, "mp", crossing)
        beyond = lax.ppermute(beyond, "mp", skipping)
        sums.append(across.astype(F32) + beyond.astype(F32))
    total = base + to_edge.astype(F32) + to_inner.astype(F32)
    total = total + jnp.concatenate(sums, axis=1)
    if len(whole) == 2:
        middle = embed_dim // 2
        turned = jnp.concatenate([total[:, middle:], total[:, :middle]], axis=1)
        total = jnp.where(seq_index == 0, total, turned)
    return total.astype(BF16)[None]


def solution(mesh):
    placed = (
        P(("dp", "seq"), "mp", None),
        P(("dp", "seq"), None, "mp"),
        P(("dp", "seq"), "mp", None),
        P(("dp", "seq")),
        P(),
        P(),
        P(),
        P(),
        P(),
        P(),
        P("seq", "mp"),
        P("mp", "seq"),
    )
    return jax.shard_map(
        on_device,
        mesh=mesh,
        in_specs=placed,
        out_specs=P(("dp", "seq"), "mp", None),
        check_vma=False,
    )
```

```python
import functools

import jax
import jax.numpy as jnp
from jax import lax
from jax.experimental import pallas as pl
from jax.experimental.pallas import tpu as pltpu
from jax.sharding import PartitionSpec as P

F32 = jnp.float32
BF16 = jnp.bfloat16
LANES = 128
COORD_ROWS = 16


def swap(value, axis, step):
    count = lax.axis_size(axis)
    return lax.ppermute(value, axis, [(i, i ^ step) for i in range(count)])


def high_low(value):
    high = value.astype(BF16)
    low = (value - high.astype(F32)).astype(BF16)
    return high, low


def in_hbm(*arrays):
    return [pltpu.with_memory_space_constraint(array, pltpu.HBM) for array in arrays]


def near_kernel(feats_ref, xyz_ref, w_near_ref, out_ref, feats, xyz, weights, arrived):
    residues = feats.shape[0]
    parts, height, depth = weights.shape
    copies = [
        pltpu.make_async_copy(feats_ref, feats, arrived.at[parts]),
        pltpu.make_async_copy(xyz_ref, xyz, arrived.at[parts + 1]),
    ] + [
        pltpu.make_async_copy(
            w_near_ref.at[part * height : (part + 1) * height, :],
            weights.at[part],
            arrived.at[part],
        )
        for part in range(parts)
    ]
    for copy in copies:
        copy.start()
    out_ref[residues:, :] = jnp.zeros((COORD_ROWS, depth), BF16)
    copies[0].wait()
    copies[1].wait()
    out_ref[residues : residues + 3, 0:residues] = xyz[...]
    near = None
    for part in range(parts):
        copies[2 + part].wait()
        term = jnp.dot(
            feats[:, part * height : (part + 1) * height],
            weights[part],
            preferred_element_type=F32,
        )
        near = term if near is None else near + term
    out_ref[0:residues, :] = near.astype(BF16)


def near_rows(feats, xyz, w_near):
    residues, depth = feats.shape
    parts = 4
    return pl.pallas_call(
        near_kernel,
        out_shape=jax.ShapeDtypeStruct((residues + COORD_ROWS, depth), BF16),
        in_specs=[pl.BlockSpec(memory_space=pltpu.HBM)] * 3,
        out_specs=pl.BlockSpec(memory_space=pltpu.VMEM),
        scratch_shapes=[
            pltpu.VMEM(feats.shape, BF16),
            pltpu.VMEM(xyz.shape, BF16),
            pltpu.VMEM((parts, depth // parts, depth), BF16),
            pltpu.SemaphoreType.DMA((parts + 2,)),
        ],
        name="near_rows",
    )(*in_hbm(feats, xyz, w_near))


def token_kernel(turn_ref, table_ref, gain_ref, w_up_ref, out_ref, scaled_ref):
    wide = table_ref[...].astype(F32)
    wide = wide - jnp.mean(wide, axis=1, keepdims=True)
    scaled = wide * gain_ref[...]
    filler = jnp.zeros((scaled_ref.shape[0] - scaled.shape[0], scaled.shape[1]), F32)
    scaled_ref[...] = jnp.concatenate([scaled, filler], axis=0).astype(BF16)
    depth = w_up_ref.shape[0]
    part = scaled_ref[:, pl.ds(pl.multiple_of(turn_ref[0] * depth, LANES), depth)]
    out_ref[...] = jnp.dot(part, w_up_ref[...], preferred_element_type=F32)


def token_rows(turn, table, gain, w_up):
    in_vmem = pl.BlockSpec(memory_space=pltpu.VMEM)
    return pl.pallas_call(
        token_kernel,
        out_shape=jax.ShapeDtypeStruct((LANES // 2, w_up.shape[1]), F32),
        in_specs=[pl.BlockSpec(memory_space=pltpu.SMEM)] + [in_vmem] * 3,
        out_specs=in_vmem,
        scratch_shapes=[pltpu.VMEM((LANES // 2, table.shape[1]), BF16)],
        name="token_rows",
    )(turn, table, gain, w_up)


def message_kernel(
    rows_at_once,
    first_row,
    with_tokens,
    *refs,
):
    if with_tokens:
        (token_gain_ref, w_up_ref), refs = refs[9:11], refs[:9] + refs[11:]
        (token_ref,), refs = refs[12:13], refs[:12] + refs[13:]
        (token_gain_buf, w_up_buf, scaled_ref), refs = refs[-3:], refs[:-3]
    message_body(
        rows_at_once,
        first_row,
        (token_gain_ref, w_up_ref, token_ref, token_gain_buf, w_up_buf, scaled_ref)
        if with_tokens
        else None,
        *refs,
    )


def message_body(
    rows_at_once,
    first_row,
    tokens,
    own_ref,
    side_ref,
    other_ref,
    feats_ref,
    link_ref,
    w_rbf_ref,
    gain_ref,
    w_logit_ref,
    table_ref,
    scalar_ref,
    shown_ref,
    coded_ref,
    window_ref,
    position_ref,
    feats_buf,
    link_buf,
    gain_buf,
    w_logit_buf,
    table_buf,
    place_ref,
    xyz_ref,
    message_ref,
    arrived,
):
    neighbour_count, residues = link_ref.shape
    bins, feature_dim = w_rbf_ref.shape
    vocab_size = table_ref.shape[0]
    window = 3 * residues
    early = []
    for slot, ref in enumerate((own_ref, side_ref, other_ref)):
        early.append(
            (ref.at[0:residues, :], window_ref.at[slot * residues : (slot + 1) * residues, :])
        )
        early.append(
            (ref.at[residues : residues + COORD_ROWS, 0:residues], position_ref.at[slot])
        )
    groups = LANES // bins
    for group in range(groups):
        place = window + group * bins
        early.append((w_rbf_ref, window_ref.at[place : place + bins, :]))
    early.append((link_ref, link_buf))
    late = [
        (feats_ref, feats_buf),
        (gain_ref, gain_buf),
        (w_logit_ref, w_logit_buf),
        (table_ref, table_buf),
    ]
    if tokens:
        token_gain_ref, w_up_ref, token_ref, token_gain_buf, w_up_buf, scaled_ref = tokens
        late += [(token_gain_ref, token_gain_buf), (w_up_ref, w_up_buf)]
    copies = [
        pltpu.make_async_copy(source, target, arrived.at[place])
        for place, (source, target) in enumerate(early + late)
    ]
    for copy in copies:
        copy.start()
    for copy in copies[: len(early)]:
        copy.wait()

    block_index = scalar_ref[0]
    residue_count = scalar_ref[1]
    positions = [position_ref[slot].astype(F32) for slot in range(3)]
    xyz_ref[...] = jnp.transpose(
        jnp.concatenate([positions[0], jnp.zeros((LANES - COORD_ROWS, residues), F32)], axis=0)
    )
    place_ref[...] = jnp.transpose(
        jnp.concatenate(
            [link_buf[...], jnp.zeros((LANES - neighbour_count, residues), jnp.int32)], axis=0
        )
    )
    lane = lax.broadcasted_iota(jnp.int32, (rows_at_once, LANES), 1)
    bin_of = jnp.bitwise_and(lane, bins - 1)
    group_of = lax.shift_right_logical(lane, bins.bit_length() - 1)
    group_short = group_of.astype(jnp.int16)
    centres = 2.0 + (20.0 / (bins - 1)) * bin_of.astype(F32)

    lane_short = lane.astype(jnp.int16)
    one, zero = jnp.ones((), BF16), jnp.zeros((), BF16)
    count = message_ref.shape[0]
    for begin in range(0, count, rows_at_once):
        first = first_row + begin
        links = place_ref[pl.ds(first, rows_at_once), :]
        keep = (links < residue_count) & (lane < neighbour_count)
        within = jnp.bitwise_and(links, residues - 1)
        block_of = lax.shift_right_logical(links, residues.bit_length() - 1)
        side_block = jnp.bitwise_xor(block_index, 1)
        slot_of = jnp.where(
            block_of == block_index, 0, jnp.where(block_of == side_block, 1, 2)
        )
        own_xyz = xyz_ref[pl.ds(first, rows_at_once), :]
        squared = None
        for slot in range(3):
            total = None
            for axis in range(3):
                offset = own_xyz[:, axis : axis + 1] - positions[slot][axis : axis + 1, :]
                total = offset * offset if total is None else total + offset * offset
            picked = jnp.take_along_axis(total, within, axis=1)
            squared = picked if squared is None else jnp.where(slot_of == slot, picked, squared)
        distance = jnp.where(keep, jnp.sqrt(squared), 1e6)
        place = jnp.where(keep, within + slot_of * residues, -1)
        rows = []
        for k in range(neighbour_count):
            place_k = jnp.broadcast_to(place[:, k : k + 1], (rows_at_once, LANES))
            place_k = place_k.astype(jnp.int16)
            parts = [
                jnp.where(place_k == lane_short + jnp.int16(slot * residues), one, zero)
                for slot in range(3)
            ]
            if k % groups == 0:
                spread_out = jnp.take_along_axis(distance, group_of + k, axis=1)
                scaled = (spread_out - centres) * (1.0 / 1.25)
                radial = jnp.exp(-scaled * scaled).astype(BF16)
            parts.append(jnp.where(group_short == jnp.int16(k % groups), radial, zero))
            rows.append(jnp.concatenate(parts, axis=1))
        selector = jnp.concatenate(rows, axis=0)
        width = 256
        for column in range(feature_dim // width):
            cols = slice(column * width, (column + 1) * width)
            preact = jnp.dot(selector, window_ref[:, cols], preferred_element_type=F32)
            doubled = preact * (1.0 + lax.erf(preact * (0.5**0.5)))
            message_ref[pl.ds(begin, rows_at_once), cols] = jnp.sum(
                doubled.reshape(neighbour_count, rows_at_once, width), axis=0
            ) * (0.5 / 30.0)

    for copy in copies[len(early) :]:
        copy.wait()
    values = feats_buf[first_row : first_row + count, :].astype(F32) + message_ref[...]
    centred = values - jnp.mean(values, axis=1, keepdims=True)
    spread = jnp.mean(centred * centred, axis=1, keepdims=True)
    mixed = (centred * lax.rsqrt(spread + 1e-5) * gain_buf[...]).astype(BF16)
    half = LANES // 2
    w_logit = jnp.concatenate(
        [w_logit_buf[...].astype(F32), jnp.zeros((LANES - vocab_size, feature_dim), F32)], axis=0
    ).astype(BF16)
    logits = lax.dot_general(
        mixed, w_logit, (((1,), (1,)), ((), ())), preferred_element_type=F32
    )
    bounded = 8.0 * jnp.tanh(logits * 0.125)
    token = lax.broadcasted_iota(jnp.int32, logits.shape, 1)
    exponent = jnp.where(token < vocab_size, jnp.exp(bounded), 0.0)
    probability = (exponent / jnp.sum(exponent, axis=1, keepdims=True)).astype(BF16)
    residue = (
        block_index * residues + first_row + lax.broadcasted_iota(jnp.int32, (count, 1), 0)
    )
    valid = (residue < residue_count).astype(F32)
    table = jnp.concatenate(
        [
            table_buf[...].astype(F32),
            jnp.zeros((LANES - vocab_size, table_buf.shape[1]), F32),
        ],
        axis=0,
    ).astype(BF16)
    soft = (jnp.dot(probability, table, preferred_element_type=F32) * valid).astype(BF16)
    shown_ref[...] = (probability.astype(F32) * valid).astype(BF16)
    soft_wide = soft.astype(F32)
    soft_centred = soft_wide - jnp.mean(soft_wide, axis=1, keepdims=True)
    soft_spread = jnp.mean(soft_centred * soft_centred, axis=1, keepdims=True)
    coded = probability.astype(F32) * (lax.rsqrt(soft_spread + 1e-5) * valid)
    high, low = high_low(coded)
    coded_ref[...] = jnp.concatenate([high[:, :half], low[:, :half]], axis=1)
    if tokens:
        wide = table.astype(F32)[:half]
        wide = wide - jnp.mean(wide, axis=1, keepdims=True)
        scaled_ref[...] = (wide * token_gain_buf[...]).astype(BF16)
        depth = w_up_buf.shape[0]
        part = scaled_ref[:, pl.ds(pl.multiple_of(scalar_ref[2] * depth, LANES), depth)]
        token_ref[...] = jnp.dot(part, w_up_buf[...], preferred_element_type=F32)


def messages(own, side, other, feats, links, w_rbf, gain, w_logit, table, scalars, rows, tokens):
    residues, feature_dim = feats.shape
    embed_dim = table.shape[1]
    bins = w_rbf.shape[0]
    depth = 3 * residues + LANES
    count = rows[1] - rows[0]
    in_vmem = pl.BlockSpec(memory_space=pltpu.VMEM)
    in_hbm_spec = pl.BlockSpec(memory_space=pltpu.HBM)
    arrays = [own, side, other, feats, links, w_rbf, gain, w_logit, table, *tokens]
    out_shape = [jax.ShapeDtypeStruct((count, LANES), BF16)] * 2
    scratch = [
        pltpu.VMEM((depth, feature_dim), BF16),
        pltpu.VMEM((3, COORD_ROWS, residues), BF16),
        pltpu.VMEM(feats.shape, BF16),
        pltpu.VMEM(links.shape, jnp.int32),
        pltpu.VMEM(gain.shape, F32),
        pltpu.VMEM(w_logit.shape, BF16),
        pltpu.VMEM(table.shape, BF16),
        pltpu.VMEM((residues, LANES), jnp.int32),
        pltpu.VMEM((residues, LANES), F32),
        pltpu.VMEM((count, feature_dim), F32),
        pltpu.SemaphoreType.DMA((12 + LANES // bins,)),
    ]
    if tokens:
        token_gain, w_up = tokens
        out_shape.append(jax.ShapeDtypeStruct((LANES // 2, w_up.shape[1]), F32))
        scratch += [
            pltpu.VMEM(token_gain.shape, F32),
            pltpu.VMEM(w_up.shape, BF16),
            pltpu.VMEM((LANES // 2, embed_dim), BF16),
        ]
    return pl.pallas_call(
        functools.partial(message_kernel, min(32, count), rows[0], bool(tokens)),
        out_shape=out_shape,
        in_specs=[in_hbm_spec] * len(arrays) + [pl.BlockSpec(memory_space=pltpu.SMEM)],
        out_specs=[in_vmem] * len(out_shape),
        scratch_shapes=scratch,
        compiler_params=pltpu.CompilerParams(vmem_limit_bytes=20 << 20),
        cost_estimate=pl.CostEstimate(
            flops=100_000_000 * count, bytes_accessed=5_000_000, transcendentals=50_000 * count
        ),
        name="messages",
    )(*in_hbm(*arrays), scalars)


def gelu_rows(rows, up):
    total = jnp.dot(rows, jnp.concatenate([up, up], axis=0), preferred_element_type=F32)
    return (0.5 * total * (1.0 + lax.erf(total * (0.5**0.5)))).astype(BF16)


def trunk_kernel(blocks, columns, targets, table_columns, *refs):
    coded, up_ref, refs = refs[:blocks], refs[blocks], refs[blocks + 1 :]
    weights, refs = refs[: len(columns)], refs[len(columns) :]
    if table_columns:
        shown_ref, turn_ref, table_ref, refs = refs[0], refs[1], refs[2], refs[3:]
        refs, (table_raw, table_buf, base_buf, extra) = refs[:-4], refs[-4:]
        base_ref, refs = refs[0], refs[1:]
        fetching = pltpu.make_async_copy(table_ref, table_raw, extra.at[0])
        fetching.start()
    outs = refs[:-3]
    inner, results, left = refs[-3:]
    chunk = results.shape[2]
    rows = coded[0].shape[0]
    for place, ref in enumerate(coded):
        inner[place * rows : (place + 1) * rows, :] = gelu_rows(ref[...], up_ref[...])
    leaving = []
    for place, (ref, first) in enumerate(zip(weights, columns)):
        value = jnp.dot(
            inner[...], ref[:, first : first + chunk], preferred_element_type=F32
        )
        if table_columns:
            if place == 0:
                fetching.wait()
                filler = (table_buf.shape[0] - table_raw.shape[0], table_raw.shape[1])
                table_buf[...] = jnp.concatenate(
                    [table_raw[...].astype(F32), jnp.zeros(filler, F32)], axis=0
                ).astype(BF16)
            half_width = table_buf.shape[1] // 2
            first = pl.multiple_of(
                lax.rem(turn_ref[0] * half_width + table_columns[place], 2 * half_width), LANES
            )
            soft = jnp.dot(
                shown_ref[...], table_buf[:, pl.ds(first, chunk)], preferred_element_type=F32
            )
            base_buf[:, place * chunk : (place + 1) * chunk] = value[
                (blocks - 1) * rows :
            ].astype(BF16).astype(F32) + soft.astype(BF16).astype(F32)
            value = value[: (blocks - 1) * rows]
        results[place] = value.astype(BF16)
        for number, (start, stop) in enumerate(targets):
            leaving.append(
                pltpu.make_async_copy(
                    results.at[place, start:stop, :],
                    outs[number].at[:, place * chunk : (place + 1) * chunk],
                    left.at[len(leaving)],
                )
            )
            leaving[-1].start()
    if table_columns:
        leaving.append(pltpu.make_async_copy(base_buf, base_ref, extra.at[1]))
        leaving[-1].start()
    for copy in leaving:
        copy.wait()


def trunk(coded, up, pieces, targets, chunk, shown=None, turn=None, table=None):
    with_base = table is not None
    kept = len(coded) - with_base
    rows, hidden = coded[0].shape[0], up.shape[1]
    in_vmem = pl.BlockSpec(memory_space=pltpu.VMEM)
    hbm_spec = pl.BlockSpec(memory_space=pltpu.HBM)
    return pl.pallas_call(
        functools.partial(
            trunk_kernel,
            len(coded),
            [column for _, column in pieces],
            targets,
            [place * chunk for place in range(len(pieces))] if with_base else (),
        ),
        out_shape=[pltpu.HBM((rows, len(pieces) * chunk), F32)] * with_base
        + [pltpu.HBM((stop - start, len(pieces) * chunk), BF16) for start, stop in targets],
        in_specs=[in_vmem] * (len(coded) + 1) + [in_vmem] * len(pieces)
        + [in_vmem, pl.BlockSpec(memory_space=pltpu.SMEM), hbm_spec] * with_base,
        out_specs=[hbm_spec] * (with_base + len(targets)),
        scratch_shapes=[
            pltpu.VMEM((len(coded) * rows, hidden), BF16),
            pltpu.VMEM((len(pieces), kept * rows, chunk), BF16),
            pltpu.SemaphoreType.DMA((len(pieces) * len(targets),)),
        ]
        + (
            [
                pltpu.VMEM(table.shape, BF16),
                pltpu.VMEM((LANES, table.shape[1]), BF16),
                pltpu.VMEM((rows, len(pieces) * chunk), F32),
                pltpu.SemaphoreType.DMA((2,)),
            ]
            if with_base
            else []
        ),
        compiler_params=pltpu.CompilerParams(vmem_limit_bytes=16 << 20),
        cost_estimate=pl.CostEstimate(
            flops=2 * len(coded) * rows * len(pieces) * hidden * chunk,
            bytes_accessed=2 * hidden * chunk * len(pieces),
            transcendentals=len(coded) * rows * hidden,
        ),
        name="trunk",
    )(
        *coded,
        up,
        *[array for array, _ in pieces],
        *((shown, turn, in_hbm(table)[0]) if with_base else ()),
    )


def rounded_sum(left, right):
    return (left.astype(F32) + right.astype(F32)).astype(BF16)


def on_device(
    node_feats,
    coords,
    neighbours,
    counts,
    w_near,
    w_rbf,
    gen_gain,
    w_logit,
    embed_table,
    trunk_gain,
    w_up,
    w_down,
):
    backbones, residues, feature_dim = node_feats.shape
    assert backbones == 1 and lax.axis_size("mp") == 4
    vocab_size, embed_dim = embed_table.shape
    half = LANES // 2
    seq_count = lax.axis_size("seq")
    seq_index = lax.axis_index("seq")
    block_index = lax.axis_index("mp")

    own = near_rows(node_feats[0], coords[0], w_near)
    side = swap(own, "mp", 1)
    other = lax.ppermute(own, "mp", [(1, 2), (2, 1)])

    scalars = jnp.stack([block_index.astype(jnp.int32), counts[0], seq_index.astype(jnp.int32)])

    in_kernel = seq_count == 2 and w_up.shape[0] % LANES == 0
    if in_kernel:
        token_up = token_rows(
            seq_index.astype(jnp.int32)[None], embed_table, trunk_gain[None, :], w_up
        )
        token_up = (token_up + swap(token_up, "seq", 1)).astype(BF16)
    shown, coded = messages(
        own,
        side,
        other,
        node_feats[0],
        neighbours[0].T,
        w_rbf,
        gen_gain[None, :],
        w_logit.T,
        embed_table,
        scalars,
        (0, residues),
        (),
    )
    if in_kernel:
        whole = [w_down] + [swap(w_down, "seq", 1)]
    else:
        table_wide = embed_table.astype(F32)
        table_centred = table_wide - jnp.mean(table_wide, axis=1, keepdims=True)
        table_scaled = jnp.pad(
            (table_centred * trunk_gain).astype(BF16), ((0, half - vocab_size), (0, 0))
        )
        table_part = lax.dynamic_slice_in_dim(
            table_scaled, seq_index * w_up.shape[0], w_up.shape[0], 1
        )
        token_up = lax.psum(
            jnp.dot(table_part, w_up, preferred_element_type=F32), "seq"
        ).astype(BF16)
        whole = [lax.all_gather(w_down, "seq", axis=1, tiled=True)]
    chunk = embed_dim // 4
    pieces = [(part, first) for part in whole for first in range(0, part.shape[1], chunk)]

    inward = [(0, 1), (3, 2)]
    crossing = [(1, 2), (2, 1)]
    skipping = [(1, 3), (2, 0)]
    coded_3, coded_2, coded_1 = [swap(coded, "mp", step) for step in (3, 2, 1)]
    coded_3, coded_2, coded_1, token_up = lax.optimization_barrier(
        (coded_3, coded_2, coded_1, token_up)
    )
    pairs = [(0, 2 * residues)]
    (far_a,) = trunk([coded_3, coded_2], token_up, pieces[:2], pairs, chunk)
    coded_1, _ = lax.optimization_barrier((coded_1, far_a))
    turn = seq_index.astype(jnp.int32) if len(whole) == 2 else jnp.zeros((), jnp.int32)
    base, near = trunk(
        [coded_1, coded],
        token_up,
        pieces,
        [(0, residues)],
        chunk,
        shown,
        turn[None],
        embed_table,
    )
    coded_3, _ = lax.optimization_barrier((coded_3, near))
    (far_b,) = trunk([coded_3, coded_2], token_up, pieces[2:], pairs, chunk)
    arrived_a = lax.ppermute(far_a, "mp", inward)
    to_edge = lax.ppermute(near, "mp", [(1, 0), (2, 3)])
    arrived_b = lax.ppermute(far_b, "mp", inward)
    arrived_a, far_a, _ = lax.optimization_barrier((arrived_a, far_a, far_b))
    near, _ = lax.optimization_barrier((near, arrived_b))
    to_inner = lax.ppermute(near, "mp", inward)
    sums = []
    for far, arrived in ((far_a, arrived_a), (far_b, arrived_b)):
        across = rounded_sum(far[:residues], arrived[residues:])
        beyond = rounded_sum(far[residues:], arrived[:residues])
        beyond = lax.ppermute(beyond, "mp", skipping)
        across = lax.ppermute(across, "mp", crossing)
        sums.append(beyond.astype(F32) + across.astype(F32))
    total = base + to_edge.astype(F32) + to_inner.astype(F32)
    total = total + jnp.concatenate(sums, axis=1)
    if len(whole) == 2:
        middle = embed_dim // 2
        turned = jnp.concatenate([total[:, middle:], total[:, :middle]], axis=1)
        total = jnp.where(seq_index == 0, total, turned)
    return total.astype(BF16)[None]


def solution(mesh):
    placed = (
        P(("dp", "seq"), "mp", None),
        P(("dp", "seq"), None, "mp"),
        P(("dp", "seq"), "mp", None),
        P(("dp", "seq")),
        P(),
        P(),
        P(),
        P(),
        P(),
        P(),
        P("seq", "mp"),
        P("mp", "seq"),
    )
    return jax.shard_map(
        on_device,
        mesh=mesh,
        in_specs=placed,
        out_specs=P(("dp", "seq"), "mp", None),
        check_vma=False,
    )
```
